256 devices in a mesh: dp: 64 (over x_lo, y, z), section: 2 (over core), tensor: 2 (over x_hi).
Axes of the slice: x: 4 (x_hi: 2, x_lo: 2; x = x_hi * 2 + x_lo), y: 4, z: 8, core: 2. Of those that a mesh axis runs over, the one named last changes fastest.
Arguments:
- tower_input: bfloat16 [2, 12288, 1024], P('section', 'dp'), may hold values from -8 to 8
- up_weight: bfloat16 [2, 1024, 4096], P('section', None, 'tensor'), may hold values from -0.1875 to 0.1875
- down_weight: bfloat16 [2, 4096, 1024], P('section', 'tensor'), may hold values from -0.09375 to 0.09375
- pair: int32 [12288], P('dp'), may hold values from 0 to 12287, each once
- scale: float32 [1], replicated, may hold values from 4 to 16
- bias: float32 [1], replicated, may hold values from -4 to -1
Outputs:
- loss: float32 [1], replicated
- slide_grad: float32 [12288, 1024], P(('dp', 'section', 'tensor'))
- report_grad: float32 [12288, 1024], P(('dp', 'section', 'tensor'))
The draws below stay inside these ranges and needn't reach their ends.
Inputs may be any that keep to these rules, and one draw needn't show every extreme that they name: `pair`: each report index appears exactly once.
All inputs are finite; a program needn't handle non-finite values.
Results may differ from the reference program's by a relative error of at most 0.00036.
Values may be sent and summed in bfloat16 or wider, within the bound.
No kernel may reach another device: no remote copies, remote signals or barrier semaphores. Data moves between devices by JAX's collectives and lax.ppermute only.
A program may use at most 128 MiB of HBM per device.

```python
import math
import jax
import jax.numpy as jnp
from jax import lax

D = 1024
H = 4096
PAIRS_DEV = 48
B = 12288


def draw_tower_input(key, part):
    key_center = jax.random.fold_in(key, 11)
    key_member = jax.random.fold_in(key, 12)
    key_strength = jax.random.fold_in(key, 13)
    key_noise = jax.random.fold_in(key, 14)
    groups = 8
    centers = jax.random.normal(key_center, (groups, D), jnp.float32)
    member = jax.random.randint(key_member, (2, B), 0, groups)
    strength = jnp.exp(jax.random.uniform(key_strength, (2, B, 1), jnp.float32, jnp.log(0.4), jnp.log(1.6)))
    noise = 0.6 * jax.random.normal(key_noise, (2, B, D), jnp.float32)
    shared = jnp.take(centers, member, axis=0) * strength
    values = jnp.clip(shared + noise, -8.0, 8.0)
    return values.astype(jnp.bfloat16)


def level_of(key, shape, split, least, top_value):
    factor_of, own = 1.0, jax.random.fold_in(key, 6)
    for dim, shards_of in split:
        heights = jnp.exp(jax.random.uniform(jax.random.fold_in(own, dim), (shards_of,), jnp.float32, least / len(split), top_value / len(split)))
        factor_of = factor_of * jnp.repeat(heights, shape[dim] // shards_of).reshape([-1 if axis == dim else 1 for axis in range(len(shape))])
    return factor_of


def scatter_about(rng, extent, scale, reach, split=(), kind=jnp.bfloat16):
    result = jax.random.normal(rng, extent, jnp.float32) * scale
    if len(split) > 0:
        result = level_of(rng, extent, split, -0.22, 0.18) * result
    return jnp.clip(result, min=-reach, max=reach).astype(kind)


def setup_inputs(seed: int = 0) -> dict:
    streams_of = jax.random.split(jax.random.key(seed), 7)
    return {
        "tower_input": draw_tower_input(jax.random.fold_in(streams_of[6], 71), 0),
        "up_weight": scatter_about(streams_of[1], (2, D, H), D ** -0.5, 0.1875, ((0, 2), (2, 2))),
        "down_weight": scatter_about(streams_of[2], (2, H, D), H ** -0.5, 0.09375, ((0, 2), (1, 2))),
        "pair": jax.random.permutation(streams_of[3], B).astype(jnp.int32),
        "scale": jnp.clip(jnp.exp(jax.random.uniform(streams_of[4], (1,), jnp.float32, math.log(4.0), math.log(16.0))), 4.0, 16.0),
        "bias": jnp.clip(jax.random.uniform(streams_of[5], (1,), jnp.float32, -4.0, -1.0), -4.0, -1.0),
    }


def tower(inputs, up_part, down_part):
    hidden = jax.nn.gelu(jnp.dot(inputs, up_part, preferred_element_type=jnp.float32)).astype(jnp.bfloat16)
    raw = inputs.astype(jnp.float32) + jnp.dot(hidden, down_part, preferred_element_type=jnp.float32)
    norms = lax.rsqrt(lax.optimization_barrier(jnp.sum(raw * raw, axis=-1, keepdims=True)) + 1e-06)
    return (raw * norms).astype(jnp.bfloat16)

def reference(tower_input, up_weight, down_weight, pair, scale, bias):
    slides = tower(tower_input[0], up_weight[0], down_weight[0])
    reports = tower(tower_input[1], up_weight[1], down_weight[1])
    total = slides.shape[0]
    block = 4 * PAIRS_DEV
    columns = jnp.arange(total, dtype=jnp.int32)

    def step(carry, index):
        loss_sum, report_sum = carry
        start = (index * block).astype(jnp.int32)
        slide_rows = lax.dynamic_slice_in_dim(slides, start, block, 0)
        pair_rows = lax.dynamic_slice_in_dim(pair, start, block, 0)
        logits = scale[0] * lax.dot_general(slide_rows, reports, (((1,), (1,)), ((), ())), preferred_element_type=jnp.float32) + bias[0]
        sign = jnp.where(pair_rows[:, None] == columns[None, :], 1.0, -1.0).astype(jnp.float32)
        loss_sum = loss_sum + jnp.sum(jnp.logaddexp(jnp.float32(0.0), -sign * logits))
        weight = (-scale[0] * sign * jax.nn.sigmoid(-sign * logits)).astype(jnp.bfloat16)
        slide_part = jnp.dot(weight, reports, preferred_element_type=jnp.float32)
        report_sum = report_sum + lax.dot_general(weight, slide_rows, (((0,), (0,)), ((), ())), preferred_element_type=jnp.float32)
        return ((loss_sum, report_sum), slide_part)
    start_carry = (jnp.zeros((), jnp.float32), jnp.zeros((total, D), jnp.float32))
    (loss_sum, report_grad), slide_parts = lax.scan(step, start_carry, jnp.arange(total // block, dtype=jnp.int32))
    loss = (loss_sum / total).reshape(1)
    return (loss, slide_parts.reshape(total, D), report_grad)
```

```python
import jax
import jax.numpy as jnp
from jax import lax
from jax.sharding import Mesh
from jax.sharding import PartitionSpec as P

DP = ("xl", "y", "z")
PLANE = ("xl", "y", "tensor")
ALL = ("xl", "y", "z", "section", "tensor")
SWAP = [(0, 1), (1, 0)]
F32 = jnp.float32
SENT = jnp.float16


def exchanged(parts, axes):
    return lax.all_to_all(parts, axes, split_axis=0, concat_axis=0, tiled=True)


def copies(array, axes):
    return exchanged(jnp.broadcast_to(array, (lax.axis_size(axes), *array.shape)), axes)


def tower(inputs, up, down, tensor):
    rows, width = inputs.shape
    split = inputs.reshape(2, 2, rows // 4, width)
    kept = lax.dynamic_slice_in_dim(split, tensor, 1, 1).reshape(rows // 2, width)
    given = lax.dynamic_slice_in_dim(split, 1 - tensor, 1, 1).reshape(rows // 2, width)
    ordered = jnp.concatenate([given, kept], axis=0)
    hidden = jax.nn.gelu(jnp.dot(ordered, up, preferred_element_type=F32)).astype(jnp.bfloat16)
    sent = jnp.dot(hidden[: rows // 2], down, preferred_element_type=F32)
    arrived = lax.ppermute(sent, "tensor", SWAP)
    own = jnp.dot(hidden[rows // 2 :], down, preferred_element_type=F32)
    raw = own + arrived + kept.astype(F32)
    norms = lax.rsqrt(jnp.sum(raw * raw, axis=-1, keepdims=True) + 1e-06)
    return (raw * norms).astype(jnp.bfloat16).reshape(2, rows // 4, width)


def local(tower_input, up_weight, down_weight, pair, scale, bias):
    section = lax.axis_index("section")
    tensor = lax.axis_index("tensor")
    n_z = lax.axis_size("z")
    n_plane = lax.axis_size(PLANE)
    scale_value, bias_value = scale[0], bias[0]
    quarter = tower_input.shape[1] // 4
    total = lax.axis_size(ALL) * quarter

    pair_rows = lax.dynamic_slice_in_dim(pair.reshape(2, 2, quarter), tensor, 1, 1)
    pair_rows = jnp.pad(pair_rows.reshape(1, 2, quarter), ((0, 0), (0, 0), (0, 128 - quarter)))
    pair_all = copies(pair_rows[0], "z")[:, :, :quarter]
    pair_own = lax.dynamic_index_in_dim(pair_all, section, 1, keepdims=False)
    pair_other = lax.dynamic_index_in_dim(pair_all, 1 - section, 1, keepdims=False)
    pair_all = jnp.concatenate([pair_own.reshape(-1), pair_other.reshape(-1)])

    embedded = tower(tower_input[0], up_weight[0], down_weight[0], tensor)
    mine = lax.dynamic_index_in_dim(embedded, section, 0, keepdims=False)
    given = lax.dynamic_index_in_dim(embedded, 1 - section, 0, keepdims=False)
    got = lax.ppermute(given, "section", SWAP)
    slides = jnp.where(section == 0, mine, got)
    reports = jnp.where(section == 0, got, mine)

    slides_z = copies(slides, "z").reshape(n_z * quarter, -1)
    reports_all = copies(reports, PLANE).reshape(n_plane * quarter, -1)
    slides_all = jnp.concatenate([slides_z, lax.ppermute(slides_z, "section", SWAP)], axis=0)

    place = jnp.arange(n_plane * quarter, dtype=jnp.int32)
    member, row = place // quarter, place % quarter
    owner = ((member // 2 * n_z + lax.axis_index("z")) * 2 + section) * 2 + member % 2
    columns = owner * quarter + row

    dots = lax.dot_general(
        slides_all, reports_all, (((1,), (1,)), ((), ())), preferred_element_type=F32
    )
    logits = scale_value * dots + bias_value
    match = pair_all[:, None] == columns[None, :]
    turned = jnp.where(match, -logits, logits)
    small = jnp.exp(-jnp.abs(turned))
    loss_part = jnp.sum(jnp.maximum(turned, 0.0) + jnp.log1p(small))
    sigmoid = jnp.where(turned >= 0, 1.0, small) / (1.0 + small)
    weight = (jnp.where(match, -scale_value, scale_value) * sigmoid).astype(jnp.bfloat16)
    slide_part = jnp.dot(weight, reports_all, preferred_element_type=F32)
    report_part = lax.dot_general(
        weight, slides_all, (((0,), (0,)), ((), ())), preferred_element_type=F32
    )
    half = n_z * quarter
    slide_half = slide_part[:half] + lax.ppermute(slide_part[half:], "section", SWAP)
    slide_terms = exchanged(slide_half.astype(SENT).reshape(n_z, quarter, -1), "z")
    report_terms = exchanged(report_part.astype(SENT).reshape(n_plane, quarter, -1), PLANE)
    slide_grad = slide_terms.astype(F32).sum(axis=0)
    report_grad = report_terms.astype(F32).sum(axis=0)

    losses = jnp.broadcast_to(loss_part, (1, 128))
    losses = losses + lax.ppermute(losses, "section", SWAP)
    losses = copies(losses, PLANE).sum(axis=0)
    losses = copies(losses, "z").sum(axis=0)
    loss = losses[0, :1] / total
    return (loss, slide_grad, report_grad)


def solution(mesh):
    finer = Mesh(
        mesh.devices.reshape(2, 4, 8, mesh.shape["section"], mesh.shape["tensor"]),
        ALL,
    )
    return jax.shard_map(
        local,
        mesh=finer,
        in_specs=(
            P("section", DP, None),
            P("section", None, "tensor"),
            P("section", "tensor", None),
            P(DP),
            P(),
            P(),
        ),
        out_specs=(P(), P(ALL, None), P(ALL, None)),
        check_vma=False,
    )
```

```python
import jax
import jax.numpy as jnp
from jax import lax
from jax.sharding import Mesh
from jax.sharding import PartitionSpec as P

DP = ("xl", "y", "z")
PLANE = ("xl", "y", "tensor")
ALL = ("xl", "y", "z", "section", "tensor")
SWAP = [(0, 1), (1, 0)]
OFFSETS = (0, -1, 1, -2, 2, -3, 3, 4)
F32 = jnp.float32
SENT = jnp.float16


def exchanged(parts, axes):
    return lax.all_to_all(parts, axes, split_axis=0, concat_axis=0, tiled=True)


def copies(array, axes):
    return exchanged(jnp.broadcast_to(array, (lax.axis_size(axes), *array.shape)), axes)


def to_offset(array, offset):
    n = lax.axis_size("z")
    return lax.ppermute(array, "z", [(i, (i + offset) % n) for i in range(n)])


def flipped(array, axis, bit):
    n = lax.axis_size(axis)
    return lax.ppermute(array, axis, [(i, i ^ bit) for i in range(n)])


def ring_gathered(own):
    below, above = to_offset(own, 1), to_offset(own, -1)
    below2, above2 = to_offset(below, 1), to_offset(above, -1)
    below3, above3 = to_offset(below2, 1), to_offset(above2, -1)
    across = to_offset(below2, 2)
    return [own, below, above, below2, above2, below3, above3, across]


def ring_summed(parts):
    own, below, above, below2, above2, below3, above3, across = parts
    up = to_offset(above3.astype(SENT), 1)
    far = to_offset(across.astype(SENT), 2)
    down = to_offset(below3.astype(SENT), -1)
    up = to_offset((above2 + up.astype(F32) + far.astype(F32)).astype(SENT), 1)
    down = to_offset((below2 + down.astype(F32)).astype(SENT), -1)
    up = to_offset((above + up.astype(F32)).astype(SENT), 1)
    down = to_offset((below + down.astype(F32)).astype(SENT), -1)
    return own + up.astype(F32) + down.astype(F32)


def summed_everywhere(value):
    value = value + flipped(value, "section", 1)
    for axis in ("tensor", "xl", "y", "z"):
        bit = 1
        while bit < lax.axis_size(axis):
            value = value + flipped(value, axis, bit)
            bit *= 2
    return value


def tower(inputs, up, down, tensor, pair_rows):
    rows, width = inputs.shape
    split = inputs.reshape(2, 2, rows // 4, width)
    kept = lax.dynamic_slice_in_dim(split, tensor, 1, 1).reshape(rows // 2, width)
    given = lax.dynamic_slice_in_dim(split, 1 - tensor, 1, 1).reshape(rows // 2, width)
    ordered = jnp.concatenate([given, kept], axis=0)
    hidden = jax.nn.gelu(jnp.dot(ordered, up, preferred_element_type=F32)).astype(jnp.bfloat16)
    sent = jnp.dot(hidden[: rows // 2], down, preferred_element_type=F32)
    arrived = lax.ppermute(sent, "tensor", SWAP)
    own = jnp.dot(hidden[rows // 2 :], down, preferred_element_type=F32) + kept.astype(F32)
    own, pair_rows = lax.optimization_barrier((own, pair_rows))
    pairs = jnp.stack(
        [pair_rows] + [to_offset(pair_rows, -offset) for offset in OFFSETS[1:]], axis=1
    )
    raw = own + arrived
    norms = lax.rsqrt(jnp.sum(raw * raw, axis=-1, keepdims=True) + 1e-06)
    return (raw * norms).astype(jnp.bfloat16).reshape(2, rows // 4, width), pairs


def local(tower_input, up_weight, down_weight, pair, scale, bias):
    section = lax.axis_index("section")
    tensor = lax.axis_index("tensor")
    n_z = lax.axis_size("z")
    n_plane = lax.axis_size(PLANE)
    scale_value, bias_value = scale[0], bias[0]
    quarter = tower_input.shape[1] // 4
    total = lax.axis_size(ALL) * quarter
    half = n_z * quarter

    pair_rows = lax.dynamic_slice_in_dim(pair.reshape(2, 2, quarter), tensor, 1, 1)
    embedded, pairs = tower(
        tower_input[0], up_weight[0], down_weight[0], tensor, pair_rows.reshape(2, quarter)
    )
    pair_mine = lax.dynamic_index_in_dim(pairs, section, 0, keepdims=False).reshape(-1)
    pair_other = lax.dynamic_index_in_dim(pairs, 1 - section, 0, keepdims=False).reshape(-1)
    pair_all = jnp.concatenate([pair_mine, pair_other])

    mine = lax.dynamic_index_in_dim(embedded, section, 0, keepdims=False)
    given = lax.dynamic_index_in_dim(embedded, 1 - section, 0, keepdims=False)
    got = lax.ppermute(given, "section", SWAP)
    slides = jnp.where(section == 0, mine, got)
    reports = jnp.where(section == 0, got, mine)

    reports_all = copies(reports, PLANE).reshape(n_plane * quarter, -1)
    slides_z = jnp.concatenate(ring_gathered(slides), axis=0)
    slides_all = jnp.concatenate([slides_z, lax.ppermute(slides_z, "section", SWAP)], axis=0)

    place = jnp.arange(n_plane * quarter, dtype=jnp.int32)
    member, row = place // quarter, place % quarter
    owner = ((member // 2 * n_z + lax.axis_index("z")) * 2 + section) * 2 + member % 2
    columns = owner * quarter + row

    dots = lax.dot_general(
        slides_all, reports_all, (((1,), (1,)), ((), ())), preferred_element_type=F32
    )
    logits = scale_value * dots + bias_value
    match = pair_all[:, None] == columns[None, :]
    turned = jnp.where(match, -logits, logits)
    small = jnp.exp(-jnp.abs(turned))
    loss_part = jnp.sum(jnp.maximum(turned, 0.0) + jnp.log1p(small))
    sigmoid = jnp.where(turned >= 0, 1.0, small) / (1.0 + small)
    weight = (jnp.where(match, -scale_value, scale_value) * sigmoid).astype(jnp.bfloat16)

    report_part = lax.dot_general(
        weight, slides_all, (((0,), (0,)), ((), ())), preferred_element_type=F32
    ).astype(SENT)
    report_part, weight, loss_part = lax.optimization_barrier((report_part, weight, loss_part))
    report_terms = exchanged(report_part.reshape(n_plane, quarter, -1), PLANE)
    slide_other = jnp.dot(weight[half:], reports_all, preferred_element_type=F32)
    slide_back = lax.ppermute(slide_other, "section", SWAP)
    slide_mine = jnp.dot(weight[:half], reports_all, preferred_element_type=F32) + slide_back
    parts = [slide_mine[k * quarter : (k + 1) * quarter] for k in range(n_z)]
    slide_grad = ring_summed(parts)
    loss = summed_everywhere(jnp.broadcast_to(loss_part, (1, 128)))[0, :1] / total
    report_grad = report_terms.astype(F32).sum(axis=0)
    return (loss, slide_grad, report_grad)


def solution(mesh):
    finer = Mesh(
        mesh.devices.reshape(2, 4, 8, mesh.shape["section"], mesh.shape["tensor"]),
        ALL,
    )
    return jax.shard_map(
        local,
        mesh=finer,
        in_specs=(
            P("section", DP, None),
            P("section", None, "tensor"),
            P("section", "tensor", None),
            P(DP),
            P(),
            P(),
        ),
        out_specs=(P(), P(ALL, None), P(ALL, None)),
        check_vma=False,
    )
```

```python
import jax
import jax.numpy as jnp
from jax import lax
from jax.sharding import Mesh
from jax.sharding import PartitionSpec as P

DP = ("xl", "y", "z")
PLANE = ("xl", "y", "tensor")
ALL = ("xl", "y", "z", "section", "tensor")
SWAP = [(0, 1), (1, 0)]
LANES = 128
F32 = jnp.float32
SENT = jnp.float16


def exchanged(parts, axes):
    return lax.all_to_all(parts, axes, split_axis=0, concat_axis=0, tiled=True)


def copies(array, axes):
    return exchanged(jnp.broadcast_to(array, (lax.axis_size(axes), *array.shape)), axes)


def to_offset(array, offset):
    n = lax.axis_size("z")
    return lax.ppermute(array, "z", [(i, (i + offset) % n) for i in range(n)])


def flipped(array, axis, bit):
    n = lax.axis_size(axis)
    return lax.ppermute(array, axis, [(i, i ^ bit) for i in range(n)])


def gathered_over_z(own):
    below, above = to_offset(own, 1), to_offset(own, -1)
    below2, above2 = to_offset(own, 2), to_offset(own, -2)
    below, above, below2, above2 = lax.optimization_barrier((below, above, below2, above2))
    cut = own.shape[0] // 2
    below3, above3 = to_offset(below2, 1), to_offset(above2, -1)
    top = to_offset(below2[:cut], 2)
    bottom = to_offset(above2[cut:], -2)
    return [own, below, above, below2, above2, below3, above3, top, bottom]


def tied(*arrays):
    return lax.optimization_barrier(arrays)


def summed_over_z(parts, value):
    own, below, above, below2, above2, below3, above3, across = parts
    cut = own.shape[0] // 2
    halves = across.astype(SENT)
    up3, down3 = to_offset(above3.astype(SENT), 1), to_offset(below3.astype(SENT), -1)
    top, bottom = to_offset(halves[:cut], 2), to_offset(halves[cut:], -2)
    up, down = to_offset(above.astype(SENT), 1), to_offset(below.astype(SENT), -1)
    other = flipped(value, "z", 1)
    up3, down3, top, bottom, up, down, other = tied(up3, down3, top, bottom, up, down, other)
    value = value + other
    up2 = above2 + up3.astype(F32)
    up2 = jnp.concatenate([up2[:cut] + top.astype(F32), up2[cut:]], axis=0)
    down2 = below2 + down3.astype(F32)
    down2 = jnp.concatenate([down2[:cut], down2[cut:] + bottom.astype(F32)], axis=0)
    up2, down2 = to_offset(up2.astype(SENT), 2), to_offset(down2.astype(SENT), -2)
    other = flipped(value, "z", 2)
    up2, down2, other = tied(up2, down2, other)
    value = value + other
    value = value + flipped(value, "z", 4)
    near = own + up.astype(F32) + down.astype(F32)
    return near + up2.astype(F32) + down2.astype(F32), value


def tower(inputs, up, down, tensor):
    rows, width = inputs.shape
    split = inputs.reshape(2, 2, rows // 4, width)
    kept = lax.dynamic_slice_in_dim(split, tensor, 1, 1).reshape(rows // 2, width)
    given = lax.dynamic_slice_in_dim(split, 1 - tensor, 1, 1).reshape(rows // 2, width)
    ordered = jnp.concatenate([given, kept], axis=0)
    hidden = jax.nn.gelu(jnp.dot(ordered, up, preferred_element_type=F32)).astype(jnp.bfloat16)
    sent = jnp.dot(hidden[: rows // 2], down, preferred_element_type=F32)
    arrived = lax.ppermute(sent, "tensor", SWAP)
    later, sent = tied(hidden[rows // 2 :], sent)
    own = jnp.dot(later, down, preferred_element_type=F32) + kept.astype(F32)
    own = lax.optimization_barrier(own)
    raw = own + arrived
    norms = lax.rsqrt(jnp.sum(raw * raw, axis=-1, keepdims=True) + 1e-06)
    return (raw * norms).astype(jnp.bfloat16).reshape(2, rows // 4, width)


def pair_lanes(pair, section, tensor, quarter):
    rows = lax.dynamic_slice_in_dim(pair, (section * 2 + tensor) * quarter, quarter)[:, None]
    lane = lax.broadcasted_iota(jnp.int32, (quarter, LANES), 1)
    digits = jnp.where(lane == 0, rows // LANES, jnp.where(lane == 1, rows % LANES, 0))
    return digits.astype(jnp.bfloat16)


def scored(rows, width, reports, columns, scale_value, bias_value):
    slides = rows[:, :width]
    wanted = rows[:, width].astype(F32) * LANES + rows[:, width + 1].astype(F32)
    dots = lax.dot_general(
        slides, reports, (((1,), (1,)), ((), ())), preferred_element_type=F32
    )
    logits = scale_value * dots + bias_value
    match = wanted[:, None] == columns[None, :]
    turned = jnp.where(match, -logits, logits)
    small = jnp.exp(-jnp.abs(turned))
    loss_part = jnp.sum(jnp.maximum(turned, 0.0) + jnp.log1p(small))
    sigmoid = jnp.where(turned >= 0, 1.0, small) / (1.0 + small)
    weight = jnp.where(match, -scale_value, scale_value) * sigmoid
    return slides, weight.astype(jnp.bfloat16), loss_part


def transposed_dot(weight, slides):
    return lax.dot_general(weight, slides, (((0,), (0,)), ((), ())), preferred_element_type=F32)


def local(tower_input, up_weight, down_weight, pair, scale, bias):
    section = lax.axis_index("section")
    tensor = lax.axis_index("tensor")
    n_z = lax.axis_size("z")
    n_plane = lax.axis_size(PLANE)
    scale_value, bias_value = scale[0], bias[0]
    quarter, width = tower_input.shape[1] // 4, tower_input.shape[2]
    total = lax.axis_size(ALL) * quarter

    lanes = pair_lanes(pair, section, tensor, quarter)
    embedded = tower(tower_input[0], up_weight[0], down_weight[0], tensor)
    mine = lax.dynamic_index_in_dim(embedded, section, 0, keepdims=False)
    given = lax.dynamic_index_in_dim(embedded, 1 - section, 0, keepdims=False)
    got = lax.ppermute(given, "section", SWAP)
    slides = jnp.concatenate([jnp.where(section == 0, mine, got), lanes], axis=1)
    reports = jnp.where(section == 0, got, mine)

    reports_all = copies(reports, PLANE).reshape(n_plane * quarter, -1)
    rows_mine = jnp.concatenate(gathered_over_z(slides), axis=0)
    rows_other = lax.ppermute(rows_mine, "section", SWAP)

    place = jnp.arange(n_plane * quarter, dtype=jnp.int32)
    member, row = place // quarter, place % quarter
    owner = ((member // 2 * n_z + lax.axis_index("z")) * 2 + section) * 2 + member % 2
    columns = (owner * quarter + row).astype(F32)

    slides_mine, weight_mine, loss_mine = scored(
        rows_mine, width, reports_all, columns, scale_value, bias_value
    )
    slides_other, weight_other, loss_other = scored(
        rows_other, width, reports_all, columns, scale_value, bias_value
    )
    loss_value = jnp.broadcast_to(loss_mine + loss_other, (1, 128))
    loss_value = copies(loss_value, PLANE).sum(axis=0)
    report_part = transposed_dot(weight_mine, slides_mine)
    report_part = (report_part + transposed_dot(weight_other, slides_other)).astype(SENT)
    report_part, weight_mine, weight_other = tied(report_part, weight_mine, weight_other)
    report_terms = exchanged(report_part.reshape(n_plane, quarter, -1), PLANE)
    slide_other = jnp.dot(weight_other, reports_all, preferred_element_type=F32)
    slide_back = lax.ppermute(slide_other, "section", SWAP)
    loss_back = lax.ppermute(loss_value, "section", SWAP)
    slide_mine = jnp.dot(weight_mine, reports_all, preferred_element_type=F32) + slide_back
    parts = [slide_mine[k * quarter : (k + 1) * quarter] for k in range(n_z)]
    slide_grad, loss_value = summed_over_z(parts, loss_value + loss_back)
    report_grad = report_terms.astype(F32).sum(axis=0)
    return (loss_value[0, :1] / total, slide_grad, report_grad)


def solution(mesh):
    finer = Mesh(
        mesh.devices.reshape(2, 4, 8, mesh.shape["section"], mesh.shape["tensor"]),
        ALL,
    )
    return jax.shard_map(
        local,
        mesh=finer,
        in_specs=(
            P("section", DP, None),
            P("section", None, "tensor"),
            P("section", "tensor", None),
            P(DP),
            P(),
            P(),
        ),
        out_specs=(P(), P(ALL, None), P(ALL, None)),
        check_vma=False,
    )
```

```python
import jax
import jax.numpy as jnp
from jax import lax
from jax.sharding import Mesh
from jax.sharding import PartitionSpec as P

DP = ("xl", "y", "z")
PLANE = ("xl", "y", "tensor")
ALL = ("xl", "y", "z", "section", "tensor")
SWAP = [(0, 1), (1, 0)]
LANES = 128
F32 = jnp.float32
SENT = jnp.float16


def exchanged(parts, axes):
    return lax.all_to_all(parts, axes, split_axis=0, concat_axis=0, tiled=True)


def copies(array, axes):
    return exchanged(jnp.broadcast_to(array, (lax.axis_size(axes), *array.shape)), axes)


def to_offset(array, offset):
    n = lax.axis_size("z")
    return lax.ppermute(array, "z", [(i, (i + offset) % n) for i in range(n)])


def flipped(array, axis, bit):
    n = lax.axis_size(axis)
    return lax.ppermute(array, axis, [(i, i ^ bit) for i in range(n)])


def gathered_over_z(own):
    cut = own.shape[0] // 2
    below, above = tied(to_offset(own, 1), to_offset(own, -1))
    below2, above2 = tied(to_offset(below, 1), to_offset(above, -1))
    top, bottom = to_offset(below2[:cut], 2), to_offset(above2[cut:], -2)
    below3, above3 = to_offset(below2, 1), to_offset(above2, -1)
    return [own, below, above, below2, above2, below3, above3, top, bottom]


def tied(*arrays):
    return lax.optimization_barrier(arrays)


def with_digits(part, value):
    high = (value / 4096.0).astype(SENT)
    value = value - high.astype(F32) * 4096.0
    middle = (value / 4.0).astype(SENT)
    low = (value - middle.astype(F32) * 4.0).astype(SENT)
    shape = (*part.shape[:-1], LANES)
    lane = lax.broadcasted_iota(jnp.int32, shape, len(shape) - 1)
    lanes = jnp.where(lane == 0, high, jnp.where(lane == 1, middle, low))
    return jnp.concatenate([part.astype(SENT), lanes], axis=-1)


def without_digits(sent):
    width = sent.shape[-1] - LANES
    lanes = sent[:, 0, width:].astype(F32).sum(axis=0)
    value = lanes[0] * 4096.0 + lanes[1] * 4.0 + lanes[2]
    return sent[..., :width].astype(F32), value


def summed_over_z(parts):
    own, below, above, below2, above2, below3, above3, across = parts
    cut = own.shape[0] // 2
    halves = across.astype(SENT)
    up3, down3 = to_offset(above3.astype(SENT), 1), to_offset(below3.astype(SENT), -1)
    up, down = to_offset(above.astype(SENT), 1), to_offset(below.astype(SENT), -1)
    top, bottom = to_offset(halves[:cut], 2), to_offset(halves[cut:], -2)
    up3, down3, top, bottom, up, down = tied(up3, down3, top, bottom, up, down)
    up2 = above2 + up3.astype(F32)
    up2 = jnp.concatenate([up2[:cut] + top.astype(F32), up2[cut:]], axis=0)
    down2 = below2 + down3.astype(F32)
    down2 = jnp.concatenate([down2[:cut], down2[cut:] + bottom.astype(F32)], axis=0)
    up2, down2 = tied(to_offset(up2.astype(SENT), 2), to_offset(down2.astype(SENT), -2))
    near = own + up.astype(F32) + down.astype(F32)
    return near + up2.astype(F32) + down2.astype(F32)


def tower(inputs, up, down, tensor):
    rows, width = inputs.shape
    split = inputs.reshape(2, 2, rows // 4, width)
    kept = lax.dynamic_slice_in_dim(split, tensor, 1, 1).reshape(rows // 2, width)
    given = lax.dynamic_slice_in_dim(split, 1 - tensor, 1, 1).reshape(rows // 2, width)
    ordered = jnp.concatenate([given, kept], axis=0)
    hidden = jax.nn.gelu(jnp.dot(ordered, up, preferred_element_type=F32)).astype(jnp.bfloat16)
    sent = jnp.dot(hidden[: rows // 2], down, preferred_element_type=F32)
    arrived = lax.ppermute(sent, "tensor", SWAP)
    later, sent = tied(hidden[rows // 2 :], sent)
    own = jnp.dot(later, down, preferred_element_type=F32) + kept.astype(F32)
    own = lax.optimization_barrier(own)
    raw = own + arrived
    norms = lax.rsqrt(jnp.sum(raw * raw, axis=-1, keepdims=True) + 1e-06)
    return (raw * norms).astype(jnp.bfloat16).reshape(2, rows // 4, width)


def pair_lanes(pair, section, tensor, quarter):
    rows = lax.dynamic_slice_in_dim(pair, (section * 2 + tensor) * quarter, quarter)[:, None]
    lane = lax.broadcasted_iota(jnp.int32, (quarter, LANES), 1)
    digits = jnp.where(lane == 0, rows // LANES, jnp.where(lane == 1, rows % LANES, 0))
    return digits.astype(jnp.bfloat16)


def scored(rows, width, reports, columns, scale_value, bias_value):
    slides = rows[:, :width]
    wanted = rows[:, width].astype(F32) * LANES + rows[:, width + 1].astype(F32)
    dots = lax.dot_general(
        slides, reports, (((1,), (1,)), ((), ())), preferred_element_type=F32
    )
    logits = scale_value * dots + bias_value
    match = wanted[:, None] == columns[None, :]
    turned = jnp.where(match, -logits, logits)
    small = jnp.exp(-jnp.abs(turned))
    loss_part = jnp.sum(jnp.maximum(turned, 0.0) + jnp.log1p(small))
    sigmoid = jnp.where(turned >= 0, 1.0, small) / (1.0 + small)
    weight = jnp.where(match, -scale_value, scale_value) * sigmoid
    return slides, weight.astype(jnp.bfloat16), loss_part


def transposed_dot(weight, slides):
    return lax.dot_general(weight, slides, (((0,), (0,)), ((), ())), preferred_element_type=F32)


def local(tower_input, up_weight, down_weight, pair, scale, bias):
    section = lax.axis_index("section")
    tensor = lax.axis_index("tensor")
    n_z = lax.axis_size("z")
    n_plane = lax.axis_size(PLANE)
    scale_value, bias_value = scale[0], bias[0]
    quarter, width = tower_input.shape[1] // 4, tower_input.shape[2]
    total = lax.axis_size(ALL) * quarter

    lanes = pair_lanes(pair, section, tensor, quarter)
    embedded = tower(tower_input[0], up_weight[0], down_weight[0], tensor)
    mine = lax.dynamic_index_in_dim(embedded, section, 0, keepdims=False)
    given = lax.dynamic_index_in_dim(embedded, 1 - section, 0, keepdims=False)
    got = lax.ppermute(given, "section", SWAP)
    slides = jnp.concatenate([jnp.where(section == 0, mine, got), lanes], axis=1)
    reports = jnp.where(section == 0, got, mine)

    repeated = jnp.broadcast_to(reports, (n_plane, *reports.shape))
    repeated, slides = tied(repeated, slides)
    reports_all = exchanged(repeated, PLANE).reshape(n_plane * quarter, -1)
    rows_mine = jnp.concatenate(gathered_over_z(slides), axis=0)
    rows_other = lax.ppermute(rows_mine, "section", SWAP)

    place = jnp.arange(n_plane * quarter, dtype=jnp.int32)
    member, row = place // quarter, place % quarter
    owner = ((member // 2 * n_z + lax.axis_index("z")) * 2 + section) * 2 + member % 2
    columns = (owner * quarter + row).astype(F32)

    slides_mine, weight_mine, loss_mine = scored(
        rows_mine, width, reports_all, columns, scale_value, bias_value
    )
    slides_other, weight_other, loss_other = scored(
        rows_other, width, reports_all, columns, scale_value, bias_value
    )
    report_part = transposed_dot(weight_mine, slides_mine)
    report_part = report_part + transposed_dot(weight_other, slides_other)
    report_part = with_digits(
        report_part.reshape(n_plane, quarter, width), loss_mine + loss_other
    )
    report_part, weight_mine, weight_other = tied(report_part, weight_mine, weight_other)
    report_terms = exchanged(report_part, PLANE)
    slide_other = jnp.dot(weight_other, reports_all, preferred_element_type=F32)
    slide_back = lax.ppermute(slide_other, "section", SWAP)
    slide_mine = jnp.dot(weight_mine, reports_all, preferred_element_type=F32) + slide_back
    parts = [slide_mine[k * quarter : (k + 1) * quarter] for k in range(n_z)]
    slide_grad = summed_over_z(parts)
    report_terms, slide_grad = tied(report_terms, slide_grad)
    report_terms, loss_value = without_digits(report_terms)
    losses = copies(jnp.broadcast_to(loss_value, (1, LANES)), ("z", "section"))
    loss = jnp.sum(losses, axis=0)[0, :1] / total
    return (loss, slide_grad, report_terms.sum(axis=0))


def solution(mesh):
    finer = Mesh(
        mesh.devices.reshape(2, 4, 8, mesh.shape["section"], mesh.shape["tensor"]),
        ALL,
    )
    return jax.shard_map(
        local,
        mesh=finer,
        in_specs=(
            P("section", DP, None),
            P("section", None, "tensor"),
            P("section", "tensor", None),
            P(DP),
            P(),
            P(),
        ),
        out_specs=(P(), P(ALL, None), P(ALL, None)),
        check_vma=False,
    )
```

```python
import jax
import jax.numpy as jnp
from jax import lax
from jax.sharding import Mesh
from jax.sharding import PartitionSpec as P

DP = ("xl", "y", "z")
PLANE = ("xl", "y", "tensor")
ALL = ("xl", "y", "z", "section", "tensor")
SWAP = [(0, 1), (1, 0)]
LANES = 128
F32 = jnp.float32
SENT = jnp.float16


def exchanged(parts, axes):
    return lax.all_to_all(parts, axes, split_axis=0, concat_axis=0, tiled=True)


def copies(array, axes):
    return exchanged(jnp.broadcast_to(array, (lax.axis_size(axes), *array.shape)), axes)


def along_z(array, chips):
    n = lax.axis_size("z")
    pairs = []
    for z in range(n):
        pairs.append((2 * z, 2 * ((z + chips) % n)))
        pairs.append((2 * z + 1, 2 * ((z - chips) % n) + 1))
    return lax.ppermute(array, ("z", "section"), pairs)


def row_half(array, which):
    half = array.shape[0] // 2
    return lax.dynamic_slice_in_dim(array, which * half, half, 0)


def gathered_over_z(own, section):
    two = along_z(own, 2)
    one_three = along_z(jnp.concatenate([own, two], axis=0), 1)
    four = along_z(row_half(two, section), 2)
    return jnp.concatenate([own, one_three, two, four], axis=0)


def tied(*arrays):
    return lax.optimization_barrier(arrays)


def with_digits(part, value):
    high = (value / 4096.0).astype(SENT)
    value = value - high.astype(F32) * 4096.0
    middle = (value / 4.0).astype(SENT)
    low = (value - middle.astype(F32) * 4.0).astype(SENT)
    shape = (*part.shape[:-1], LANES)
    lane = lax.broadcasted_iota(jnp.int32, shape, len(shape) - 1)
    lanes = jnp.where(lane == 0, high, jnp.where(lane == 1, middle, low))
    return jnp.concatenate([part.astype(SENT), lanes], axis=-1)


def without_digits(sent):
    width = sent.shape[-1] - LANES
    lanes = sent[:, 0, width:].astype(F32).sum(axis=0)
    value = lanes[0] * 4096.0 + lanes[1] * 4.0 + lanes[2]
    return sent[..., :width].astype(F32), value


def summed_over_z(kept, section):
    half = kept.shape[0] // 8
    one_three = along_z(kept[: 4 * half].astype(SENT), -1)
    four = along_z(kept[6 * half : 7 * half].astype(SENT), -2)
    one_three, four = tied(one_three, four)
    four = four.astype(F32)
    upper = kept[4 * half : 5 * half] + jnp.where(section == 0, four, 0.0)
    lower = kept[5 * half : 6 * half] + jnp.where(section == 0, 0.0, four)
    two = jnp.concatenate([upper, lower], axis=0) + one_three[2 * half :].astype(F32)
    two = along_z(two.astype(SENT), -2).astype(F32)
    given = row_half(one_three[: 2 * half], 1 - section).astype(F32) + row_half(two, 1 - section)
    got = lax.ppermute(given, "section", SWAP)
    mine = row_half(one_three[: 2 * half], section).astype(F32) + row_half(two, section)
    return kept[7 * half :] + mine + got


def tower(inputs, up, down, tensor):
    rows, width = inputs.shape
    split = inputs.reshape(2, 2, rows // 4, width)
    kept = lax.dynamic_slice_in_dim(split, tensor, 1, 1).reshape(rows // 2, width)
    given = lax.dynamic_slice_in_dim(split, 1 - tensor, 1, 1).reshape(rows // 2, width)
    ordered = jnp.concatenate([given, kept], axis=0)
    hidden = jax.nn.gelu(jnp.dot(ordered, up, preferred_element_type=F32)).astype(jnp.bfloat16)
    sent = jnp.dot(hidden[: rows // 2], down, preferred_element_type=F32)
    arrived = lax.ppermute(sent, "tensor", SWAP)
    later, sent = tied(hidden[rows // 2 :], sent)
    own = jnp.dot(later, down, preferred_element_type=F32) + kept.astype(F32)
    own = lax.optimization_barrier(own)
    raw = own + arrived
    norms = lax.rsqrt(jnp.sum(raw * raw, axis=-1, keepdims=True) + 1e-06)
    return (raw * norms).astype(jnp.bfloat16)


def pair_lanes(pair, tensor, quarter):
    rows = lax.dynamic_slice_in_dim(pair.reshape(2, 2, quarter), tensor, 1, 1)
    rows = rows.reshape(2 * quarter, 1)
    lane = lax.broadcasted_iota(jnp.int32, (2 * quarter, LANES), 1)
    digits = jnp.where(lane == 0, rows // LANES, jnp.where(lane == 1, rows % LANES, 0))
    return digits.astype(jnp.bfloat16)


def scored(rows, width, reports, columns, scale_value, bias_value):
    slides = rows[:, :width]
    wanted = rows[:, width].astype(F32) * LANES + rows[:, width + 1].astype(F32)
    dots = lax.dot_general(
        slides, reports, (((1,), (1,)), ((), ())), preferred_element_type=F32
    )
    logits = scale_value * dots + bias_value
    match = wanted[:, None] == columns[None, :]
    turned = jnp.where(match, -logits, logits)
    small = jnp.exp(-jnp.abs(turned))
    loss_part = jnp.sum(jnp.maximum(turned, 0.0) + jnp.log1p(small))
    sigmoid = jnp.where(turned >= 0, 1.0, small) / (1.0 + small)
    weight = jnp.where(match, -scale_value, scale_value) * sigmoid
    return slides, weight.astype(jnp.bfloat16), loss_part


def transposed_dot(weight, slides):
    return lax.dot_general(weight, slides, (((0,), (0,)), ((), ())), preferred_element_type=F32)


def local(tower_input, up_weight, down_weight, pair, scale, bias):
    section = lax.axis_index("section")
    tensor = lax.axis_index("tensor")
    n_z = lax.axis_size("z")
    n_plane = lax.axis_size(PLANE)
    scale_value, bias_value = scale[0], bias[0]
    quarter, width = tower_input.shape[1] // 4, tower_input.shape[2]
    total = lax.axis_size(ALL) * quarter

    lanes = pair_lanes(pair, tensor, quarter)
    embedded = tower(tower_input[0], up_weight[0], down_weight[0], tensor)
    swapped = lax.ppermute(embedded, "section", SWAP)
    slides = jnp.concatenate([jnp.where(section == 0, embedded, swapped), lanes], axis=1)
    reports = row_half(jnp.where(section == 0, swapped, embedded), section)

    repeated = jnp.broadcast_to(reports, (n_plane, *reports.shape))
    repeated, slides = tied(repeated, slides)
    reports_all = exchanged(repeated, PLANE).reshape(n_plane * quarter, -1)
    rows_mine = gathered_over_z(slides, section)
    rows_other = lax.ppermute(rows_mine[2 * quarter :], "section", SWAP)

    place = jnp.arange(n_plane * quarter, dtype=jnp.int32)
    member, row = place // quarter, place % quarter
    owner = ((member // 2 * n_z + lax.axis_index("z")) * 2 + section) * 2 + member % 2
    columns = (owner * quarter + row).astype(F32)

    slides_mine, weight_mine, loss_mine = scored(
        rows_mine, width, reports_all, columns, scale_value, bias_value
    )
    slides_other, weight_other, loss_other = scored(
        rows_other, width, reports_all, columns, scale_value, bias_value
    )
    loss_value = jnp.broadcast_to(loss_mine + loss_other, (1, LANES))
    loss_value = copies(loss_value, ("z", "section")).sum(axis=0)[0, 0]
    report_part = transposed_dot(weight_mine, slides_mine)
    report_part = report_part + transposed_dot(weight_other, slides_other)
    report_part = with_digits(report_part.reshape(n_plane, quarter, width), loss_value)
    report_part, weight_mine, weight_other = tied(report_part, weight_mine, weight_other)
    report_terms = exchanged(report_part, PLANE)
    weight_own, weight_mine = weight_mine[: 2 * quarter], weight_mine[2 * quarter :]
    weight_sent = jnp.concatenate([weight_other, row_half(weight_own, 1 - section)], axis=0)
    weight_kept = jnp.concatenate([weight_mine, row_half(weight_own, section)], axis=0)
    sent = jnp.dot(weight_sent, reports_all, preferred_element_type=F32)
    back = lax.ppermute(sent, "section", SWAP)
    kept = jnp.dot(weight_kept, reports_all, preferred_element_type=F32) + back
    slide_grad = summed_over_z(kept, section)
    report_terms, loss_value = without_digits(report_terms)
    return (jnp.reshape(loss_value / total, (1,)), slide_grad, report_terms.sum(axis=0))


def solution(mesh):
    finer = Mesh(
        mesh.devices.reshape(2, 4, 8, mesh.shape["section"], mesh.shape["tensor"]),
        ALL,
    )
    return jax.shard_map(
        local,
        mesh=finer,
        in_specs=(
            P("section", DP, None),
            P("section", None, "tensor"),
            P("section", "tensor", None),
            P(DP),
            P(),
            P(),
        ),
        out_specs=(P(), P(ALL, None), P(ALL, None)),
        check_vma=False,
    )
```

```python
import jax
import jax.numpy as jnp
from jax import lax
from jax.sharding import Mesh
from jax.sharding import PartitionSpec as P

DP = ("xl", "y", "z")
PLANE = ("xl", "y", "tensor")
ALL = ("xl", "y", "z", "section", "tensor")
SWAP = [(0, 1), (1, 0)]
LANES = 128
F32 = jnp.float32
SENT = jnp.float16


def exchanged(parts, axes):
    return lax.all_to_all(parts, axes, split_axis=0, concat_axis=0, tiled=True)


def copies(array, axes):
    return exchanged(jnp.broadcast_to(array, (lax.axis_size(axes), *array.shape)), axes)


def along_z(array, chips):
    n = lax.axis_size("z")
    pairs = []
    for z in range(n):
        pairs.append((2 * z, 2 * ((z + chips) % n)))
        pairs.append((2 * z + 1, 2 * ((z - chips) % n) + 1))
    return lax.ppermute(array, ("z", "section"), pairs)


def row_half(array, which):
    half = array.shape[0] // 2
    return lax.dynamic_slice_in_dim(array, which * half, half, 0)


def gathered_over_z(own, section):
    two = along_z(own, 2)
    one_three = along_z(jnp.concatenate([own, two], axis=0), 1)
    four = along_z(row_half(two, section), 2)
    return jnp.concatenate([own, one_three, two, four], axis=0)


def tied(*arrays):
    return lax.optimization_barrier(arrays)


def with_partner(value, axis, bit):
    pairs = [(i, i ^ bit) for i in range(lax.axis_size(axis))]
    return value + lax.ppermute(value, axis, pairs)


def summed_over_z(kept, section, loss):
    half = kept.shape[0] // 8
    one_three = along_z(kept[: 4 * half].astype(SENT), -1)
    four = along_z(kept[6 * half : 7 * half].astype(SENT), -2)
    loss = with_partner(with_partner(loss, "y", 1), "y", 2)
    one_three, four, loss = tied(one_three, four, loss)
    four = four.astype(F32)
    upper = kept[4 * half : 5 * half] + jnp.where(section == 0, four, 0.0)
    lower = kept[5 * half : 6 * half] + jnp.where(section == 0, 0.0, four)
    two = jnp.concatenate([upper, lower], axis=0) + one_three[2 * half :].astype(F32)
    two = along_z(two.astype(SENT), -2)
    loss = with_partner(loss, "z", 1)
    two, loss = tied(two, loss)
    two = two.astype(F32)
    given = row_half(one_three[: 2 * half], 1 - section).astype(F32) + row_half(two, 1 - section)
    got = lax.ppermute(given, "section", SWAP)
    loss = with_partner(with_partner(loss, "z", 2), "z", 4)
    mine = row_half(one_three[: 2 * half], section).astype(F32) + row_half(two, section)
    return kept[7 * half :] + mine + got, loss


def tower(inputs, up, down, tensor):
    rows, width = inputs.shape
    split = inputs.reshape(2, 2, rows // 4, width)
    kept = lax.dynamic_slice_in_dim(split, tensor, 1, 1).reshape(rows // 2, width)
    given = lax.dynamic_slice_in_dim(split, 1 - tensor, 1, 1).reshape(rows // 2, width)
    ordered = jnp.concatenate([given, kept], axis=0)
    hidden = jax.nn.gelu(jnp.dot(ordered, up, preferred_element_type=F32)).astype(jnp.bfloat16)
    sent = jnp.dot(hidden[: rows // 2], down, preferred_element_type=F32)
    arrived = lax.ppermute(sent, "tensor", SWAP)
    later, sent = tied(hidden[rows // 2 :], sent)
    own = jnp.dot(later, down, preferred_element_type=F32) + kept.astype(F32)
    own = lax.optimization_barrier(own)
    raw = own + arrived
    norms = lax.rsqrt(jnp.sum(raw * raw, axis=-1, keepdims=True) + 1e-06)
    return (raw * norms).astype(jnp.bfloat16)


def pair_lanes(pair, tensor, quarter):
    rows = lax.dynamic_slice_in_dim(pair.reshape(2, 2, quarter), tensor, 1, 1)
    rows = rows.reshape(2 * quarter, 1)
    lane = lax.broadcasted_iota(jnp.int32, (2 * quarter, LANES), 1)
    digits = jnp.where(lane == 0, rows // LANES, jnp.where(lane == 1, rows % LANES, 0))
    return digits.astype(jnp.bfloat16)


def scored(rows, width, reports, columns, scale_value, bias_value):
    slides = rows[:, :width]
    wanted = rows[:, width].astype(F32) * LANES + rows[:, width + 1].astype(F32)
    dots = lax.dot_general(
        slides, reports, (((1,), (1,)), ((), ())), preferred_element_type=F32
    )
    logits = scale_value * dots + bias_value
    match = wanted[:, None] == columns[None, :]
    turned = jnp.where(match, -logits, logits)
    small = jnp.exp(-jnp.abs(turned))
    loss_part = jnp.sum(jnp.maximum(turned, 0.0) + jnp.log1p(small))
    sigmoid = jnp.where(turned >= 0, 1.0, small) / (1.0 + small)
    weight = jnp.where(match, -scale_value, scale_value) * sigmoid
    return slides, weight.astype(jnp.bfloat16), loss_part


def transposed_dot(weight, slides):
    return lax.dot_general(weight, slides, (((0,), (0,)), ((), ())), preferred_element_type=F32)


def local(tower_input, up_weight, down_weight, pair, scale, bias):
    section = lax.axis_index("section")
    tensor = lax.axis_index("tensor")
    n_z = lax.axis_size("z")
    n_plane = lax.axis_size(PLANE)
    scale_value, bias_value = scale[0], bias[0]
    quarter, width = tower_input.shape[1] // 4, tower_input.shape[2]
    total = lax.axis_size(ALL) * quarter

    lanes = pair_lanes(pair, tensor, quarter)
    embedded = tower(tower_input[0], up_weight[0], down_weight[0], tensor)
    swapped = lax.ppermute(embedded, "section", SWAP)
    slides = jnp.concatenate([jnp.where(section == 0, embedded, swapped), lanes], axis=1)
    reports = row_half(jnp.where(section == 0, swapped, embedded), section)

    repeated = jnp.broadcast_to(reports, (n_plane, *reports.shape))
    repeated, slides = tied(repeated, slides)
    reports_all = exchanged(repeated, PLANE).reshape(n_plane * quarter, -1)
    rows_mine = gathered_over_z(slides, section)
    rows_other = lax.ppermute(rows_mine[2 * quarter :], "section", SWAP)

    place = jnp.arange(n_plane * quarter, dtype=jnp.int32)
    member, row = place // quarter, place % quarter
    owner = ((member // 2 * n_z + lax.axis_index("z")) * 2 + section) * 2 + member % 2
    columns = (owner * quarter + row).astype(F32)

    slides_mine, weight_mine, loss_mine = scored(
        rows_mine, width, reports_all, columns, scale_value, bias_value
    )
    slides_other, weight_other, loss_other = scored(
        rows_other, width, reports_all, columns, scale_value, bias_value
    )
    loss = with_partner(jnp.broadcast_to(loss_mine + loss_other, (1, LANES)), "section", 1)
    report_part = transposed_dot(weight_mine, slides_mine)
    report_part = report_part + transposed_dot(weight_other, slides_other)
    report_part = report_part.astype(SENT).reshape(n_plane, quarter, width)
    report_part, weight_mine, weight_other, loss = tied(
        report_part, weight_mine, weight_other, loss
    )
    report_terms = exchanged(report_part, PLANE)
    loss = with_partner(loss, "tensor", 1)
    weight_own, weight_mine = weight_mine[: 2 * quarter], weight_mine[2 * quarter :]
    weight_sent = jnp.concatenate([weight_other, row_half(weight_own, 1 - section)], axis=0)
    weight_kept = jnp.concatenate([weight_mine, row_half(weight_own, section)], axis=0)
    sent = jnp.dot(weight_sent, reports_all, preferred_element_type=F32)
    sent, loss = tied(sent, loss)
    back = lax.ppermute(sent, "section", SWAP)
    loss = with_partner(loss, "xl", 1)
    kept = jnp.dot(weight_kept, reports_all, preferred_element_type=F32) + back
    kept, loss = tied(kept, loss)
    slide_grad, loss = summed_over_z(kept, section, loss)
    report_grad = report_terms.astype(F32).sum(axis=0)
    return (loss[0, :1] / total, slide_grad, report_grad)


def solution(mesh):
    finer = Mesh(
        mesh.devices.reshape(2, 4, 8, mesh.shape["section"], mesh.shape["tensor"]),
        ALL,
    )
    return jax.shard_map(
        local,
        mesh=finer,
        in_specs=(
            P("section", DP, None),
            P("section", None, "tensor"),
            P("section", "tensor", None),
            P(DP),
            P(),
            P(),
        ),
        out_specs=(P(), P(ALL, None), P(ALL, None)),
        check_vma=False,
    )
```

```python
import jax
import jax.numpy as jnp
from jax import lax
from jax.sharding import Mesh
from jax.sharding import PartitionSpec as P

DP = ("xl", "y", "z")
PLANE = ("xl", "y", "tensor")
ALL = ("xl", "y", "z", "section", "tensor")
SWAP = [(0, 1), (1, 0)]
LANES = 128
F32 = jnp.float32
SENT = jnp.float16


def exchanged(parts, axes):
    return lax.all_to_all(parts, axes, split_axis=0, concat_axis=0, tiled=True)


def copies(array, axes):
    return exchanged(jnp.broadcast_to(array, (lax.axis_size(axes), *array.shape)), axes)


def along_z(array, chips):
    n = lax.axis_size("z")
    pairs = []
    for z in range(n):
        pairs.append((2 * z, 2 * ((z + chips) % n)))
        pairs.append((2 * z + 1, 2 * ((z - chips) % n) + 1))
    return lax.ppermute(array, ("z", "section"), pairs)


def row_half(array, which):
    half = array.shape[0] // 2
    return lax.dynamic_slice_in_dim(array, which * half, half, 0)


def gathered_over_z(own, section):
    two = along_z(own, 2)
    one_three = along_z(jnp.concatenate([own, two], axis=0), 1)
    four = along_z(row_half(two, section), 2)
    return jnp.concatenate([own, one_three, two, four], axis=0)


def tied(*arrays):
    return lax.optimization_barrier(arrays)


def with_partner(value, axis, bit):
    pairs = [(i, i ^ bit) for i in range(lax.axis_size(axis))]
    return value + lax.ppermute(value, axis, pairs)


def summed_over_z(kept, section, loss):
    half = kept.shape[0] // 8
    one_three = along_z(kept[: 4 * half].astype(SENT), -1)
    four = along_z(kept[6 * half : 7 * half].astype(SENT), -2)
    loss = with_partner(with_partner(loss, "z", 1), "z", 2)
    one_three, four, loss = tied(one_three, four, loss)
    four = four.astype(F32)
    upper = kept[4 * half : 5 * half] + jnp.where(section == 0, four, 0.0)
    lower = kept[5 * half : 6 * half] + jnp.where(section == 0, 0.0, four)
    two = jnp.concatenate([upper, lower], axis=0) + one_three[2 * half :].astype(F32)
    two = along_z(two.astype(SENT), -2)
    loss = with_partner(loss, "z", 4)
    two, loss = tied(two, loss)
    two = two.astype(F32)
    given = row_half(one_three[: 2 * half], 1 - section).astype(F32) + row_half(two, 1 - section)
    got = lax.ppermute(given, "section", SWAP)
    loss = with_partner(with_partner(loss, "y", 1), "y", 2)
    mine = row_half(one_three[: 2 * half], section).astype(F32) + row_half(two, section)
    return kept[7 * half :] + mine + got, loss


def tower(inputs, up, down, tensor):
    rows, width = inputs.shape
    split = inputs.reshape(2, 2, rows // 4, width)
    kept = lax.dynamic_slice_in_dim(split, tensor, 1, 1).reshape(rows // 2, width)
    given = lax.dynamic_slice_in_dim(split, 1 - tensor, 1, 1).reshape(rows // 2, width)
    ordered = jnp.concatenate([given, kept], axis=0)
    hidden = jax.nn.gelu(jnp.dot(ordered, up, preferred_element_type=F32)).astype(jnp.bfloat16)
    sent = jnp.dot(hidden[: rows // 2], down, preferred_element_type=F32)
    arrived = lax.ppermute(sent, "tensor", SWAP)
    later, sent = tied(hidden[rows // 2 :], sent)
    own = jnp.dot(later, down, preferred_element_type=F32) + kept.astype(F32)
    own = lax.optimization_barrier(own)
    raw = own + arrived
    norms = lax.rsqrt(jnp.sum(raw * raw, axis=-1, keepdims=True) + 1e-06)
    return (raw * norms).astype(jnp.bfloat16)


def pair_lanes(pair, tensor, quarter):
    rows = lax.dynamic_slice_in_dim(pair.reshape(2, 2, quarter), tensor, 1, 1)
    rows = rows.reshape(2 * quarter, 1)
    lane = lax.broadcasted_iota(jnp.int32, (2 * quarter, LANES), 1)
    digits = jnp.where(lane == 0, rows // LANES, jnp.where(lane == 1, rows % LANES, 0))
    return digits.astype(jnp.bfloat16)


def scored(rows, width, reports, columns, scale_value, bias_value):
    slides = rows[:, :width]
    wanted = rows[:, width].astype(F32) * LANES + rows[:, width + 1].astype(F32)
    dots = lax.dot_general(
        slides, reports, (((1,), (1,)), ((), ())), preferred_element_type=F32
    )
    logits = scale_value * dots + bias_value
    match = wanted[:, None] == columns[None, :]
    turned = jnp.where(match, -logits, logits)
    small = jnp.exp(-jnp.abs(turned))
    loss_part = jnp.sum(jnp.maximum(turned, 0.0) + jnp.log1p(small))
    sigmoid = jnp.where(turned >= 0, 1.0, small) / (1.0 + small)
    weight = jnp.where(match, -scale_value, scale_value) * sigmoid
    return slides, weight.astype(jnp.bfloat16), loss_part


def transposed_dot(weight, slides):
    return lax.dot_general(weight, slides, (((0,), (0,)), ((), ())), preferred_element_type=F32)


def local(tower_input, up_weight, down_weight, pair, scale, bias):
    section = lax.axis_index("section")
    tensor = lax.axis_index("tensor")
    n_z = lax.axis_size("z")
    n_plane = lax.axis_size(PLANE)
    scale_value, bias_value = scale[0], bias[0]
    quarter, width = tower_input.shape[1] // 4, tower_input.shape[2]
    total = lax.axis_size(ALL) * quarter

    lanes = pair_lanes(pair, tensor, quarter)
    embedded = tower(tower_input[0], up_weight[0], down_weight[0], tensor)
    swapped = lax.ppermute(embedded, "section", SWAP)
    slides = jnp.concatenate([jnp.where(section == 0, embedded, swapped), lanes], axis=1)
    reports = row_half(jnp.where(section == 0, swapped, embedded), section)

    repeated = jnp.broadcast_to(reports, (n_plane, *reports.shape))
    repeated, slides = tied(repeated, slides)
    reports_all = exchanged(repeated, PLANE).reshape(n_plane * quarter, -1)
    rows_mine = gathered_over_z(slides, section)
    rows_other = lax.ppermute(rows_mine[2 * quarter :], "section", SWAP)

    place = jnp.arange(n_plane * quarter, dtype=jnp.int32)
    member, row = place // quarter, place % quarter
    owner = ((member // 2 * n_z + lax.axis_index("z")) * 2 + section) * 2 + member % 2
    columns = (owner * quarter + row).astype(F32)

    slides_mine, weight_mine, loss_mine = scored(
        rows_mine, width, reports_all, columns, scale_value, bias_value
    )
    slides_other, weight_other, loss_other = scored(
        rows_other, width, reports_all, columns, scale_value, bias_value
    )
    loss = with_partner(jnp.broadcast_to(loss_mine + loss_other, (1, LANES)), "tensor", 1)
    report_part = transposed_dot(weight_mine, slides_mine)
    report_part = report_part + transposed_dot(weight_other, slides_other)
    report_part = report_part.astype(SENT).reshape(n_plane, quarter, width)
    report_part, weight_mine, weight_other, loss = tied(
        report_part, weight_mine, weight_other, loss
    )
    report_terms = exchanged(report_part, PLANE)
    loss = with_partner(loss, "xl", 1)
    weight_own, weight_mine = weight_mine[: 2 * quarter], weight_mine[2 * quarter :]
    weight_sent = jnp.concatenate([weight_other, row_half(weight_own, 1 - section)], axis=0)
    weight_kept = jnp.concatenate([weight_mine, row_half(weight_own, section)], axis=0)
    sent = jnp.dot(weight_sent, reports_all, preferred_element_type=F32)
    sent, loss = tied(sent, loss)
    back = lax.ppermute(sent, "section", SWAP)
    loss = with_partner(loss, "section", 1)
    back, loss = tied(back, loss)
    kept = jnp.dot(weight_kept, reports_all, preferred_element_type=F32) + back
    slide_grad, loss = summed_over_z(kept, section, loss)
    report_grad = report_terms.astype(F32).sum(axis=0)
    return (loss[0, :1] / total, slide_grad, report_grad)


def solution(mesh):
    finer = Mesh(
        mesh.devices.reshape(2, 4, 8, mesh.shape["section"], mesh.shape["tensor"]),
        ALL,
    )
    return jax.shard_map(
        local,
        mesh=finer,
        in_specs=(
            P("section", DP, None),
            P("section", None, "tensor"),
            P("section", "tensor", None),
            P(DP),
            P(),
            P(),
        ),
        out_specs=(P(), P(ALL, None), P(ALL, None)),
        check_vma=False,
    )
```

```python
import jax
import jax.numpy as jnp
from jax import lax
from jax.sharding import Mesh
from jax.sharding import PartitionSpec as P
from jax.experimental import pallas as pl
from jax.experimental.pallas import tpu as pltpu

DP = ("xl", "y", "z")
PLANE = ("xl", "y", "tensor")
ALL = ("xl", "y", "z", "section", "tensor")
SWAP = [(0, 1), (1, 0)]
LANES = 128
F32 = jnp.float32
SENT = jnp.float16


def exchanged(parts, axes):
    return lax.all_to_all(parts, axes, split_axis=0, concat_axis=0, tiled=True)


def copies(array, axes):
    return exchanged(jnp.broadcast_to(array, (lax.axis_size(axes), *array.shape)), axes)


def along_z(array, chips):
    n = lax.axis_size("z")
    pairs = []
    for z in range(n):
        pairs.append((2 * z, 2 * ((z + chips) % n)))
        pairs.append((2 * z + 1, 2 * ((z - chips) % n) + 1))
    return lax.ppermute(array, ("z", "section"), pairs)


def row_half(array, which):
    half = array.shape[0] // 2
    return lax.dynamic_slice_in_dim(array, which * half, half, 0)


def gathered_over_z(own, section):
    two = along_z(own, 2)
    one_three = along_z(jnp.concatenate([own, two], axis=0), 1)
    four = along_z(row_half(two, section), 2)
    return jnp.concatenate([own, one_three, two, four], axis=0)


def tied(*arrays):
    return lax.optimization_barrier(arrays)


def with_partner(value, axis, bit):
    pairs = [(i, i ^ bit) for i in range(lax.axis_size(axis))]
    return value + lax.ppermute(value, axis, pairs)


def tower(inputs, up, down, tensor):
    rows, width = inputs.shape
    split = inputs.reshape(2, 2, rows // 4, width)
    kept = lax.dynamic_slice_in_dim(split, tensor, 1, 1).reshape(rows // 2, width)
    given = lax.dynamic_slice_in_dim(split, 1 - tensor, 1, 1).reshape(rows // 2, width)
    ordered = jnp.concatenate([given, kept], axis=0)
    hidden = jax.nn.gelu(jnp.dot(ordered, up, preferred_element_type=F32)).astype(jnp.bfloat16)
    sent = jnp.dot(hidden[: rows // 2], down, preferred_element_type=F32)
    arrived = lax.ppermute(sent, "tensor", SWAP)
    later, sent = tied(hidden[rows // 2 :], sent)
    own = jnp.dot(later, down, preferred_element_type=F32) + kept.astype(F32)
    own = lax.optimization_barrier(own)
    raw = own + arrived
    norms = lax.rsqrt(jnp.sum(raw * raw, axis=-1, keepdims=True) + 1e-06)
    return (raw * norms).astype(jnp.bfloat16)


def pair_lanes(pair, tensor, quarter):
    rows = lax.dynamic_slice_in_dim(pair.reshape(2, 2, quarter), tensor, 1, 1)
    rows = rows.reshape(2 * quarter, 1)
    lane = lax.broadcasted_iota(jnp.int32, (2 * quarter, LANES), 1)
    digits = jnp.where(lane == 0, rows // LANES, jnp.where(lane == 1, rows % LANES, 0))
    return digits.astype(jnp.bfloat16)


def score_kernel(
    spot, scale, bias, mine, other, reports, columns, weight, moved, sent, loss
):
    count, width = reports.shape
    scale_value, bias_value = scale[0], bias[0]
    z, section = spot[0], spot[1]
    toward = 2 * section - 1
    quarter = mine.shape[0] // 9
    half = 8 * quarter

    def place(step, own):
        row = lax.rem(z + toward * step + 8, 8) * quarter
        return pl.multiple_of(row + (1 - own) * half, 16)

    blocks = []
    for step in (0, 1, 3, 2):
        blocks += [(step, 1 - section), (step, section)]
    blocks.append((4, 1))
    for step in (-1, -3, -2):
        blocks += [(step, 1 - section), (step, section)]
    blocks.append((4, 0))

    total = jnp.zeros((1, count), F32)
    block = 0
    for rows, sizes in ((mine, (4, 5)), (other, (4, 3))):
        start = 0
        for size in sizes:
            stop = start + size * quarter
            marks = rows[start:stop, width : width + 2].astype(F32)
            wanted = marks[:, 0:1] * LANES + marks[:, 1:2]
            dots = lax.dot_general(
                rows[start:stop, :width],
                reports[...],
                (((1,), (1,)), ((), ())),
                preferred_element_type=F32,
            )
            logits = scale_value * dots + bias_value
            match = wanted == columns[...]
            turned = jnp.where(match, -logits, logits)
            small = jnp.exp(-jnp.abs(turned))
            losses = jnp.maximum(turned, 0.0) + jnp.log1p(small)
            total = total + jnp.sum(losses, axis=0, keepdims=True)
            sigmoid = jnp.where(turned >= 0, 1.0, small) / (1.0 + small)
            signed = jnp.where(match, -scale_value, scale_value) * sigmoid
            signed = signed.astype(jnp.bfloat16)
            weight[block * quarter : (block + size) * quarter, :] = signed
            for k in range(size):
                part = signed[k * quarter : (k + 1) * quarter]
                moved[pl.ds(place(*blocks[block + k]), quarter), :] = part
            start, block = stop, block + size
    sent[...] = jnp.dot(moved[half:, :], reports[...], preferred_element_type=F32)
    loss[...] = jnp.broadcast_to(jnp.sum(total, axis=1, keepdims=True), loss.shape)


def scored(scale, bias, mine, other, reports, columns):
    count, width = reports.shape
    rows = mine.shape[0] + other.shape[0]
    spot = jnp.stack([lax.axis_index("z"), lax.axis_index("section")]).astype(jnp.int32)
    scalar = pl.BlockSpec(memory_space=pltpu.SMEM)
    whole = pl.BlockSpec(memory_space=pltpu.VMEM)
    return pl.pallas_call(
        score_kernel,
        in_specs=[scalar, scalar, scalar, whole, whole, whole, whole],
        out_specs=[whole, whole, whole, whole],
        out_shape=[
            jax.ShapeDtypeStruct((rows, count), jnp.bfloat16),
            jax.ShapeDtypeStruct((rows, count), jnp.bfloat16),
            jax.ShapeDtypeStruct((rows // 2, width), F32),
            jax.ShapeDtypeStruct((1, LANES), F32),
        ],
        compiler_params=pltpu.CompilerParams(vmem_limit_bytes=48 * 1024 * 1024),
        name="scores",
    )(spot, scale, bias, mine, other, reports, columns)


def transposed_dot(weight, slides):
    return lax.dot_general(weight, slides, (((0,), (0,)), ((), ())), preferred_element_type=F32)


def local(tower_input, up_weight, down_weight, pair, scale, bias):
    section = lax.axis_index("section")
    tensor = lax.axis_index("tensor")
    n_z = lax.axis_size("z")
    n_plane = lax.axis_size(PLANE)
    quarter, width = tower_input.shape[1] // 4, tower_input.shape[2]
    total = lax.axis_size(ALL) * quarter

    lanes = pair_lanes(pair, tensor, quarter)
    embedded = tower(tower_input[0], up_weight[0], down_weight[0], tensor)
    swapped = lax.ppermute(embedded, "section", SWAP)
    slides = jnp.concatenate([jnp.where(section == 0, embedded, swapped), lanes], axis=1)
    reports = row_half(jnp.where(section == 0, swapped, embedded), section)

    repeated = jnp.broadcast_to(reports, (n_plane, *reports.shape))
    repeated, slides = tied(repeated, slides)
    reports_all = exchanged(repeated, PLANE).reshape(n_plane * quarter, -1)
    rows_mine = gathered_over_z(slides, section)
    rows_other = lax.ppermute(rows_mine[2 * quarter :], "section", SWAP)

    place = jnp.arange(n_plane * quarter, dtype=jnp.int32)
    member, row = place // quarter, place % quarter
    owner = ((member // 2 * n_z + lax.axis_index("z")) * 2 + section) * 2 + member % 2
    columns = (owner * quarter + row).astype(F32)

    weight, moved, sent, loss = scored(
        scale, bias, rows_mine, rows_other, reports_all, columns[None, :]
    )
    back = lax.ppermute(sent, "section", SWAP)
    loss = with_partner(loss, "tensor", 1)
    kept = jnp.dot(moved[: sent.shape[0]], reports_all, preferred_element_type=F32)
    kept, weight = tied(kept, weight)
    slide_grad = lax.psum_scatter(kept + back, "z", tiled=True)
    loss = with_partner(loss, "xl", 1)
    cut = rows_mine.shape[0]
    report_part = transposed_dot(weight[:cut], rows_mine[:, :width])
    report_part = report_part + transposed_dot(weight[cut:], rows_other[:, :width])
    report_part = report_part.astype(SENT).reshape(n_plane, quarter, width)
    report_part, loss = tied(report_part, loss)
    report_terms = exchanged(report_part, PLANE)
    loss = with_partner(loss, "section", 1)
    for bit in (1, 2, 4):
        loss = with_partner(loss, "z", bit)
    report_terms, loss = tied(report_terms, loss)
    loss = with_partner(with_partner(loss, "y", 1), "y", 2)
    report_grad = report_terms.astype(F32).sum(axis=0)
    return (loss[0, :1] / total, slide_grad, report_grad)


def solution(mesh):
    finer = Mesh(
        mesh.devices.reshape(2, 4, 8, mesh.shape["section"], mesh.shape["tensor"]),
        ALL,
    )
    return jax.shard_map(
        local,
        mesh=finer,
        in_specs=(
            P("section", DP, None),
            P("section", None, "tensor"),
            P("section", "tensor", None),
            P(DP),
            P(),
            P(),
        ),
        out_specs=(P(), P(ALL, None), P(ALL, None)),
        check_vma=False,
    )
```

```python
import jax
import jax.numpy as jnp
from jax import lax
from jax.sharding import Mesh
from jax.sharding import PartitionSpec as P
from jax.experimental import pallas as pl
from jax.experimental.pallas import tpu as pltpu

DP = ("xl", "y", "z")
PLANE = ("xl", "y", "tensor")
ALL = ("xl", "y", "z", "section", "tensor")
SWAP = [(0, 1), (1, 0)]
LANES = 128
STEP = 512
F32 = jnp.float32
SENT = jnp.float16


def exchanged(parts, axes):
    return lax.all_to_all(parts, axes, split_axis=0, concat_axis=0, tiled=True)


def copies(array, axes):
    return exchanged(jnp.broadcast_to(array, (lax.axis_size(axes), *array.shape)), axes)


def along_z(array, chips):
    n = lax.axis_size("z")
    pairs = []
    for z in range(n):
        pairs.append((2 * z, 2 * ((z + chips) % n)))
        pairs.append((2 * z + 1, 2 * ((z - chips) % n) + 1))
    return lax.ppermute(array, ("z", "section"), pairs)


def row_half(array, which):
    half = array.shape[0] // 2
    return lax.dynamic_slice_in_dim(array, which * half, half, 0)


def gathered_over_z(own, section):
    two = along_z(own, 2)
    one_three = along_z(jnp.concatenate([own, two], axis=0), 1)
    four = along_z(row_half(two, section), 2)
    return jnp.concatenate([own, one_three, two, four], axis=0)


def tied(*arrays):
    return lax.optimization_barrier(arrays)


def with_digits(part, value):
    high = (value / 4096.0).astype(SENT)
    value = value - high.astype(F32) * 4096.0
    middle = (value / 4.0).astype(SENT)
    low = (value - middle.astype(F32) * 4.0).astype(SENT)
    shape = (*part.shape[:-1], LANES)
    lane = lax.broadcasted_iota(jnp.int32, shape, len(shape) - 1)
    lanes = jnp.where(lane == 0, high, jnp.where(lane == 1, middle, low))
    return jnp.concatenate([part.astype(SENT), lanes], axis=-1)


def without_digits(sent):
    width = sent.shape[-1] - LANES
    lanes = sent[:, 0, width:].astype(F32).sum(axis=0)
    value = lanes[0] * 4096.0 + lanes[1] * 4.0 + lanes[2]
    return sent[..., :width].astype(F32), value


def summed_over_z(kept, section):
    half = kept.shape[0] // 8
    one_three = along_z(kept[: 4 * half].astype(SENT), -1)
    four = along_z(kept[6 * half : 7 * half].astype(SENT), -2)
    one_three, four = tied(one_three, four)
    four = four.astype(F32)
    upper = kept[4 * half : 5 * half] + jnp.where(section == 0, four, 0.0)
    lower = kept[5 * half : 6 * half] + jnp.where(section == 0, 0.0, four)
    two = jnp.concatenate([upper, lower], axis=0) + one_three[2 * half :].astype(F32)
    two = along_z(two.astype(SENT), -2).astype(F32)
    given = row_half(one_three[: 2 * half], 1 - section).astype(F32) + row_half(two, 1 - section)
    got = lax.ppermute(given, "section", SWAP)
    mine = row_half(one_three[: 2 * half], section).astype(F32) + row_half(two, section)
    return kept[7 * half :] + mine + got


def tower_kernel(spot, inputs, up, down, sent, own, ordered, up_held, down_held, sems):
    quarter = inputs.shape[0] // 4
    tensor = spot[0]
    step = STEP
    count = up.shape[1] // step
    loads = []
    for k, which in enumerate((1 - tensor, 3 - tensor, tensor, 2 + tensor)):
        start = pl.multiple_of(which * quarter, 16)
        rows = pl.ds(k * quarter, quarter)
        loads.append(
            pltpu.make_async_copy(
                inputs.at[pl.ds(start, quarter), :], ordered.at[rows, :], sems.at[k]
            )
        )
    for k in range(count):
        part = pl.ds(k * step, step)
        loads.append(
            pltpu.make_async_copy(up.at[:, part], up_held.at[:, part], sems.at[4 + 2 * k])
        )
        loads.append(
            pltpu.make_async_copy(down.at[part, :], down_held.at[part, :], sems.at[5 + 2 * k])
        )
    for load in loads:
        load.start()
    for load in loads[:4]:
        load.wait()
    total = jnp.zeros((4 * quarter, inputs.shape[1]), F32)
    for k in range(count):
        loads[4 + 2 * k].wait()
        hidden = jnp.dot(
            ordered[...], up_held[:, k * step : (k + 1) * step], preferred_element_type=F32
        )
        hidden = jax.nn.gelu(hidden).astype(jnp.bfloat16)
        loads[5 + 2 * k].wait()
        total = total + jnp.dot(
            hidden, down_held[k * step : (k + 1) * step, :], preferred_element_type=F32
        )
    sent[...] = total[: 2 * quarter]
    own[...] = total[2 * quarter :] + ordered[2 * quarter :, :].astype(F32)


def tower(inputs, up, down, tensor):
    rows, width = inputs.shape
    units = up.shape[1]
    out = jax.ShapeDtypeStruct((rows // 2, width), F32)
    stays = pl.BlockSpec(memory_space=pltpu.HBM)
    sent, own = pl.pallas_call(
        tower_kernel,
        in_specs=[pl.BlockSpec(memory_space=pltpu.SMEM), stays, stays, stays],
        out_specs=[pl.BlockSpec(memory_space=pltpu.VMEM)] * 2,
        out_shape=[out, out],
        scratch_shapes=[
            pltpu.VMEM((rows, width), jnp.bfloat16),
            pltpu.VMEM((width, units), jnp.bfloat16),
            pltpu.VMEM((units, width), jnp.bfloat16),
            pltpu.SemaphoreType.DMA((4 + 2 * (units // STEP),)),
        ],
        compiler_params=pltpu.CompilerParams(vmem_limit_bytes=20 * 1024 * 1024),
        name="tower",
    )(
        jnp.reshape(tensor, (1,)).astype(jnp.int32),
        *(pltpu.with_memory_space_constraint(x, pltpu.HBM) for x in (inputs, up, down)),
    )
    raw = own + lax.ppermute(sent, "tensor", SWAP)
    norms = lax.rsqrt(jnp.sum(raw * raw, axis=-1, keepdims=True) + 1e-06)
    return (raw * norms).astype(jnp.bfloat16)


def pair_lanes(pair, tensor, quarter):
    rows = lax.dynamic_slice_in_dim(pair.reshape(2, 2, quarter), tensor, 1, 1)
    rows = rows.reshape(2 * quarter, 1)
    lane = lax.broadcasted_iota(jnp.int32, (2 * quarter, LANES), 1)
    digits = jnp.where(lane == 0, rows // LANES, jnp.where(lane == 1, rows % LANES, 0))
    return digits.astype(jnp.bfloat16)


def score_kernel(
    spot, scale, bias, mine, other, reports, columns, kept, sent, report_part, loss, weight, moved
):
    count, width = reports.shape
    scale_value, bias_value = scale[0], bias[0]
    section = spot[0]
    quarter = mine.shape[0] // 9
    half = 8 * quarter
    own_rows = pl.multiple_of(half - quarter + section * half, 16)
    other_rows = pl.multiple_of(half - quarter + (1 - section) * half, 16)
    blocks = [own_rows, other_rows]
    blocks += [k * quarter for k in range(7)] + [half + k * quarter for k in range(7)]

    total = jnp.zeros((1, count), F32)
    block = 0
    for rows, sizes in ((mine, (4, 5)), (other, (4, 3))):
        start = 0
        for size in sizes:
            stop = start + size * quarter
            marks = rows[start:stop, width : width + 2].astype(F32)
            wanted = marks[:, 0:1] * LANES + marks[:, 1:2]
            dots = lax.dot_general(
                rows[start:stop, :width],
                reports[...],
                (((1,), (1,)), ((), ())),
                preferred_element_type=F32,
            )
            logits = scale_value * dots + bias_value
            match = wanted == columns[...]
            turned = jnp.where(match, -logits, logits)
            small = jnp.exp(-jnp.abs(turned))
            losses = jnp.maximum(turned, 0.0) + jnp.log1p(small)
            total = total + jnp.sum(losses, axis=0, keepdims=True)
            sigmoid = jnp.where(turned >= 0, 1.0, small) / (1.0 + small)
            signed = jnp.where(match, -scale_value, scale_value) * sigmoid
            signed = signed.astype(jnp.bfloat16)
            weight[block * quarter : (block + size) * quarter, :] = signed
            for k in range(size):
                part = signed[k * quarter : (k + 1) * quarter]
                moved[pl.ds(blocks[block + k], quarter), :] = part
            start, block = stop, block + size
    sent[...] = jnp.dot(moved[half:, :], reports[...], preferred_element_type=F32)
    kept[...] = moved[:half, :]
    cut = mine.shape[0]
    report_part[...] = transposed_dot(weight[:cut, :], mine[:, :width])
    report_part[...] += transposed_dot(weight[cut:, :], other[:, :width])
    loss[...] = jnp.broadcast_to(jnp.sum(total, axis=1, keepdims=True), loss.shape)


def scored(scale, bias, mine, other, reports, columns):
    count, width = reports.shape
    rows = mine.shape[0] + other.shape[0]
    spot = jnp.reshape(lax.axis_index("section"), (1,)).astype(jnp.int32)
    scalar = pl.BlockSpec(memory_space=pltpu.SMEM)
    whole = pl.BlockSpec(memory_space=pltpu.VMEM)
    return pl.pallas_call(
        score_kernel,
        in_specs=[scalar, scalar, scalar, whole, whole, whole, whole],
        out_specs=[whole, whole, whole, whole],
        out_shape=[
            jax.ShapeDtypeStruct((rows // 2, count), jnp.bfloat16),
            jax.ShapeDtypeStruct((rows // 2, width), F32),
            jax.ShapeDtypeStruct((count, width), F32),
            jax.ShapeDtypeStruct((1, LANES), F32),
        ],
        scratch_shapes=[
            pltpu.VMEM((rows, count), jnp.bfloat16),
            pltpu.VMEM((rows, count), jnp.bfloat16),
        ],
        compiler_params=pltpu.CompilerParams(vmem_limit_bytes=20 * 1024 * 1024),
        name="scores",
    )(spot, scale, bias, mine, other, reports, columns)


def transposed_dot(weight, slides):
    return lax.dot_general(weight, slides, (((0,), (0,)), ((), ())), preferred_element_type=F32)


def local(tower_input, up_weight, down_weight, pair, scale, bias):
    section = lax.axis_index("section")
    tensor = lax.axis_index("tensor")
    n_z = lax.axis_size("z")
    n_plane = lax.axis_size(PLANE)
    quarter, width = tower_input.shape[1] // 4, tower_input.shape[2]
    total = lax.axis_size(ALL) * quarter

    lanes = pair_lanes(pair, tensor, quarter)
    embedded = tower(tower_input[0], up_weight[0], down_weight[0], tensor)
    swapped = lax.ppermute(embedded, "section", SWAP)
    slides = jnp.concatenate([jnp.where(section == 0, embedded, swapped), lanes], axis=1)
    reports = row_half(jnp.where(section == 0, swapped, embedded), section)

    repeated = jnp.broadcast_to(reports, (n_plane, *reports.shape))
    repeated, slides = tied(repeated, slides)
    reports_all = exchanged(repeated, PLANE).reshape(n_plane * quarter, -1)
    rows_mine = gathered_over_z(slides, section)
    rows_other = lax.ppermute(rows_mine[2 * quarter :], "section", SWAP)

    place = jnp.arange(n_plane * quarter, dtype=jnp.int32)
    member, row = place // quarter, place % quarter
    owner = ((member // 2 * n_z + lax.axis_index("z")) * 2 + section) * 2 + member % 2
    columns = (owner * quarter + row).astype(F32)

    weight, sent, report_part, loss = scored(
        scale, bias, rows_mine, rows_other, reports_all, columns[None, :]
    )
    report_part = with_digits(report_part.reshape(n_plane, quarter, width), loss[0, 0])
    back = lax.ppermute(sent, "section", SWAP)
    report_part, weight = tied(report_part, weight)
    report_terms = exchanged(report_part, PLANE)
    kept = jnp.dot(weight, reports_all, preferred_element_type=F32) + back
    slide_grad = summed_over_z(kept, section)
    report_terms, slide_grad = tied(report_terms, slide_grad)
    report_terms, loss_value = without_digits(report_terms)
    losses = copies(jnp.broadcast_to(loss_value, (1, LANES)), ("z", "section"))
    loss = jnp.sum(losses, axis=0)[0, :1] / total
    return (loss, slide_grad, report_terms.sum(axis=0))


def solution(mesh):
    finer = Mesh(
        mesh.devices.reshape(2, 4, 8, mesh.shape["section"], mesh.shape["tensor"]),
        ALL,
    )
    return jax.shard_map(
        local,
        mesh=finer,
        in_specs=(
            P("section", DP, None),
            P("section", None, "tensor"),
            P("section", "tensor", None),
            P(DP),
            P(),
            P(),
        ),
        out_specs=(P(), P(ALL, None), P(ALL, None)),
        check_vma=False,
    )
```

```python
import jax
import jax.numpy as jnp
from jax import lax
from jax.sharding import Mesh
from jax.sharding import PartitionSpec as P
from jax.experimental import pallas as pl
from jax.experimental.pallas import tpu as pltpu

DP = ("xl", "y", "z")
PLANE = ("xl", "y", "tensor")
ALL = ("xl", "y", "z", "section", "tensor")
SWAP = [(0, 1), (1, 0)]
LANES = 128
STEP = 512
F32 = jnp.float32
SENT = jnp.float16


def exchanged(parts, axes):
    return lax.all_to_all(parts, axes, split_axis=0, concat_axis=0, tiled=True)


def copies(array, axes):
    return exchanged(jnp.broadcast_to(array, (lax.axis_size(axes), *array.shape)), axes)


def along_z(array, chips):
    n = lax.axis_size("z")
    pairs = []
    for z in range(n):
        pairs.append((2 * z, 2 * ((z + chips) % n)))
        pairs.append((2 * z + 1, 2 * ((z - chips) % n) + 1))
    return lax.ppermute(array, ("z", "section"), pairs)


def row_half(array, which):
    half = array.shape[0] // 2
    return lax.dynamic_slice_in_dim(array, which * half, half, 0)


def gathered_over_z(own, section, reports):
    two = along_z(own, 2)
    two_swapped = lax.ppermute(two, "section", SWAP)
    one_three = along_z(jnp.concatenate([own, two], axis=0), 1)
    four = along_z(row_half(two, section), 2)
    one_three, four = tied(one_three, four)
    others = [lax.ppermute(one_three, "section", SWAP), two_swapped]
    others.append(lax.ppermute(four, "section", SWAP))
    return [one_three, two, four, *others], reports


def tied(*arrays):
    return lax.optimization_barrier(arrays)


def with_partner(value, axis, bit):
    pairs = [(i, i ^ bit) for i in range(lax.axis_size(axis))]
    return value + lax.ppermute(value, axis, pairs)


def summed_over_z(kept, section, loss):
    half = kept.shape[0] // 8
    one_three = along_z(kept[: 4 * half].astype(SENT), -1)
    four = along_z(kept[6 * half : 7 * half].astype(SENT), -2)
    loss = with_partner(with_partner(loss, "z", 1), "z", 2)
    one_three, four, loss = tied(one_three, four, loss)
    four = four.astype(F32)
    upper = kept[4 * half : 5 * half] + jnp.where(section == 0, four, 0.0)
    lower = kept[5 * half : 6 * half] + jnp.where(section == 0, 0.0, four)
    two = jnp.concatenate([upper, lower], axis=0) + one_three[2 * half :].astype(F32)
    two = along_z(two.astype(SENT), -2)
    loss = with_partner(loss, "z", 4)
    two, loss = tied(two, loss)
    two = two.astype(F32)
    given = row_half(one_three[: 2 * half], 1 - section).astype(F32) + row_half(two, 1 - section)
    got = lax.ppermute(given, "section", SWAP)
    loss = with_partner(with_partner(loss, "y", 1), "y", 2)
    mine = row_half(one_three[: 2 * half], section).astype(F32) + row_half(two, section)
    return kept[7 * half :] + mine + got, loss


def tower_kernel(spot, inputs, up, down, sent, own, ordered, up_held, down_held, sems):
    quarter = inputs.shape[0] // 4
    tensor = spot[0]
    step = STEP
    count = up.shape[1] // step
    loads = []
    for k, which in enumerate((1 - tensor, 3 - tensor, tensor, 2 + tensor)):
        start = pl.multiple_of(which * quarter, 16)
        rows = pl.ds(k * quarter, quarter)
        loads.append(
            pltpu.make_async_copy(
                inputs.at[pl.ds(start, quarter), :], ordered.at[rows, :], sems.at[k]
            )
        )
    for k in range(count):
        part = pl.ds(k * step, step)
        loads.append(
            pltpu.make_async_copy(up.at[:, part], up_held.at[:, part], sems.at[4 + 2 * k])
        )
        loads.append(
            pltpu.make_async_copy(down.at[part, :], down_held.at[part, :], sems.at[5 + 2 * k])
        )
    for load in loads:
        load.start()
    for load in loads[:4]:
        load.wait()
    total = jnp.zeros((4 * quarter, inputs.shape[1]), F32)
    for k in range(count):
        loads[4 + 2 * k].wait()
        hidden = jnp.dot(
            ordered[...], up_held[:, k * step : (k + 1) * step], preferred_element_type=F32
        )
        hidden = jax.nn.gelu(hidden).astype(jnp.bfloat16)
        loads[5 + 2 * k].wait()
        total = total + jnp.dot(
            hidden, down_held[k * step : (k + 1) * step, :], preferred_element_type=F32
        )
    sent[...] = total[: 2 * quarter]
    own[...] = total[2 * quarter :] + ordered[2 * quarter :, :].astype(F32)


def tower(inputs, up, down, tensor):
    rows, width = inputs.shape
    units = up.shape[1]
    out = jax.ShapeDtypeStruct((rows // 2, width), F32)
    stays = pl.BlockSpec(memory_space=pltpu.HBM)
    sent, own = pl.pallas_call(
        tower_kernel,
        in_specs=[pl.BlockSpec(memory_space=pltpu.SMEM), stays, stays, stays],
        out_specs=[pl.BlockSpec(memory_space=pltpu.VMEM)] * 2,
        out_shape=[out, out],
        scratch_shapes=[
            pltpu.VMEM((rows, width), jnp.bfloat16),
            pltpu.VMEM((width, units), jnp.bfloat16),
            pltpu.VMEM((units, width), jnp.bfloat16),
            pltpu.SemaphoreType.DMA((4 + 2 * (units // STEP),)),
        ],
        compiler_params=pltpu.CompilerParams(vmem_limit_bytes=20 * 1024 * 1024),
        name="tower",
    )(
        jnp.reshape(tensor, (1,)).astype(jnp.int32),
        *(pltpu.with_memory_space_constraint(x, pltpu.HBM) for x in (inputs, up, down)),
    )
    raw = own + lax.ppermute(sent, "tensor", SWAP)
    norms = lax.rsqrt(jnp.sum(raw * raw, axis=-1, keepdims=True) + 1e-06)
    return (raw * norms).astype(jnp.bfloat16)


def pair_lanes(pair, tensor, quarter):
    rows = lax.dynamic_slice_in_dim(pair.reshape(2, 2, quarter), tensor, 1, 1)
    rows = rows.reshape(2 * quarter, 1)
    lane = lax.broadcasted_iota(jnp.int32, (2 * quarter, LANES), 1)
    digits = jnp.where(lane == 0, rows // LANES, jnp.where(lane == 1, rows % LANES, 0))
    return digits.astype(jnp.bfloat16)


def score_kernel(
    spot, scale, bias, own, one_three, two, four, one_three_other, two_other, four_other,
    reports, columns, kept, sent, report_part, loss, rows, weight,
):
    count, width = reports.shape
    scale_value, bias_value = scale[0], bias[0]
    section = spot[0]
    quarter = own.shape[0] // 2
    place = 0
    groups = (
        (one_three, two, four, section),
        (one_three_other, two_other, four_other, 1 - section),
    )
    for group in groups:
        for part in group[:3]:
            rows[place : place + part.shape[0], :] = part[...]
            place += part.shape[0]
        start = pl.multiple_of(group[3] * quarter, 16)
        rows[place : place + quarter, :] = own[pl.ds(start, quarter), :]
        place += quarter

    total = jnp.zeros((1, count), F32)
    step = place // 4
    for k in range(4):
        start, stop = k * step, (k + 1) * step
        marks = rows[start:stop, width : width + 2].astype(F32)
        wanted = marks[:, 0:1] * LANES + marks[:, 1:2]
        dots = lax.dot_general(
            rows[start:stop, :width],
            reports[...],
            (((1,), (1,)), ((), ())),
            preferred_element_type=F32,
        )
        logits = scale_value * dots + bias_value
        match = wanted == columns[...]
        turned = jnp.where(match, -logits, logits)
        small = jnp.exp(-jnp.abs(turned))
        losses = jnp.maximum(turned, 0.0) + jnp.log1p(small)
        total = total + jnp.sum(losses, axis=0, keepdims=True)
        sigmoid = jnp.where(turned >= 0, 1.0, small) / (1.0 + small)
        signed = jnp.where(match, -scale_value, scale_value) * sigmoid
        weight[start:stop, :] = signed.astype(jnp.bfloat16)
    half = 2 * step
    loss[...] = jnp.broadcast_to(jnp.sum(total, axis=1, keepdims=True), loss.shape)
    kept[...] = weight[:half, :]
    sent[...] = jnp.dot(weight[half:, :], reports[...], preferred_element_type=F32)
    report_part[...] = transposed_dot(weight[...], rows[:, :width])


def scored(scale, bias, own, pieces, reports, columns):
    count, width = reports.shape
    rows = own.shape[0] + sum(piece.shape[0] for piece in pieces)
    spot = jnp.reshape(lax.axis_index("section"), (1,)).astype(jnp.int32)
    scalar = pl.BlockSpec(memory_space=pltpu.SMEM)
    whole = pl.BlockSpec(memory_space=pltpu.VMEM)
    return pl.pallas_call(
        score_kernel,
        in_specs=[scalar] * 3 + [whole] * 9,
        out_specs=[whole, whole, whole, whole],
        out_shape=[
            jax.ShapeDtypeStruct((rows // 2, count), jnp.bfloat16),
            jax.ShapeDtypeStruct((rows // 2, width), F32),
            jax.ShapeDtypeStruct((count, width), F32),
            jax.ShapeDtypeStruct((1, LANES), F32),
        ],
        scratch_shapes=[
            pltpu.VMEM((rows, own.shape[1]), jnp.bfloat16),
            pltpu.VMEM((rows, count), jnp.bfloat16),
        ],
        compiler_params=pltpu.CompilerParams(vmem_limit_bytes=20 * 1024 * 1024),
        name="scores",
    )(spot, scale, bias, own, *pieces, reports, columns)


def transposed_dot(weight, slides):
    return lax.dot_general(weight, slides, (((0,), (0,)), ((), ())), preferred_element_type=F32)


def local(tower_input, up_weight, down_weight, pair, scale, bias):
    section = lax.axis_index("section")
    tensor = lax.axis_index("tensor")
    n_z = lax.axis_size("z")
    n_plane = lax.axis_size(PLANE)
    quarter, width = tower_input.shape[1] // 4, tower_input.shape[2]
    total = lax.axis_size(ALL) * quarter

    lanes = pair_lanes(pair, tensor, quarter)
    embedded = tower(tower_input[0], up_weight[0], down_weight[0], tensor)
    swapped = lax.ppermute(embedded, "section", SWAP)
    slides = jnp.concatenate([jnp.where(section == 0, embedded, swapped), lanes], axis=1)
    reports = row_half(jnp.where(section == 0, swapped, embedded), section)

    repeated = jnp.broadcast_to(reports, (n_plane, *reports.shape))
    repeated, slides = tied(repeated, slides)
    reports_all = exchanged(repeated, PLANE).reshape(n_plane * quarter, -1)
    pieces, reports_all = gathered_over_z(slides, section, reports_all)

    place = jnp.arange(n_plane * quarter, dtype=jnp.int32)
    member, row = place // quarter, place % quarter
    owner = ((member // 2 * n_z + lax.axis_index("z")) * 2 + section) * 2 + member % 2
    columns = (owner * quarter + row).astype(F32)

    weight, sent, report_part, loss = scored(
        scale, bias, slides, pieces, reports_all, columns[None, :]
    )
    back = lax.ppermute(sent, "section", SWAP)
    loss = with_partner(loss, "tensor", 1)
    report_part = report_part.astype(SENT).reshape(n_plane, quarter, width)
    report_part, loss = tied(report_part, loss)
    loss = with_partner(loss, "xl", 1)
    report_part, loss, weight = tied(report_part, loss, weight)
    report_terms = exchanged(report_part, PLANE)
    loss = with_partner(loss, "section", 1)
    back, loss = tied(back, loss)
    kept = jnp.dot(weight, reports_all, preferred_element_type=F32) + back
    slide_grad, loss = summed_over_z(kept, section, loss)
    report_grad = report_terms.astype(F32).sum(axis=0)
    return (loss[0, :1] / total, slide_grad, report_grad)


def solution(mesh):
    finer = Mesh(
        mesh.devices.reshape(2, 4, 8, mesh.shape["section"], mesh.shape["tensor"]),
        ALL,
    )
    return jax.shard_map(
        local,
        mesh=finer,
        in_specs=(
            P("section", DP, None),
            P("section", None, "tensor"),
            P("section", "tensor", None),
            P(DP),
            P(),
            P(),
        ),
        out_specs=(P(), P(ALL, None), P(ALL, None)),
        check_vma=False,
    )
```

```python
import jax
import jax.numpy as jnp
from jax import lax
from jax.sharding import Mesh
from jax.sharding import PartitionSpec as P
from jax.experimental import pallas as pl
from jax.experimental.pallas import tpu as pltpu

DP = ("xl", "y", "z")
PLANE = ("xl", "y", "tensor")
ALL = ("xl", "y", "z", "section", "tensor")
SWAP = [(0, 1), (1, 0)]
LANES = 128
STEP = 512
F32 = jnp.float32
SENT = jnp.float16


def exchanged(parts, axes):
    return lax.all_to_all(parts, axes, split_axis=0, concat_axis=0, tiled=True)


def copies(array, axes):
    return exchanged(jnp.broadcast_to(array, (lax.axis_size(axes), *array.shape)), axes)


def along_z(array, chips):
    n = lax.axis_size("z")
    pairs = []
    for z in range(n):
        pairs.append((2 * z, 2 * ((z + chips) % n)))
        pairs.append((2 * z + 1, 2 * ((z - chips) % n) + 1))
    return lax.ppermute(array, ("z", "section"), pairs)


def row_half(array, which):
    half = array.shape[0] // 2
    return lax.dynamic_slice_in_dim(array, which * half, half, 0)


def gathered_over_z(own, section, reports):
    two = along_z(own, 2)
    two_swapped = lax.ppermute(two, "section", SWAP)
    one_three = along_z(jnp.concatenate([own, two], axis=0), 1)
    four = along_z(row_half(two, section), 2)
    one_three, four = tied(one_three, four)
    others = [lax.ppermute(one_three, "section", SWAP), two_swapped]
    others.append(lax.ppermute(four, "section", SWAP))
    return [one_three, two, four, *others], reports


def tied(*arrays):
    return lax.optimization_barrier(arrays)


def with_partner(value, axis, bit):
    pairs = [(i, i ^ bit) for i in range(lax.axis_size(axis))]
    return value + lax.ppermute(value, axis, pairs)


def summed_over_z(kept, section, loss):
    half = kept.shape[0] // 8
    one_three = along_z(kept[: 4 * half].astype(SENT), -1)
    four = along_z(kept[6 * half : 7 * half].astype(SENT), -2)
    loss = with_partner(with_partner(loss, "z", 1), "z", 2)
    one_three, four, loss = tied(one_three, four, loss)
    four = four.astype(F32)
    upper = kept[4 * half : 5 * half] + jnp.where(section == 0, four, 0.0)
    lower = kept[5 * half : 6 * half] + jnp.where(section == 0, 0.0, four)
    two = jnp.concatenate([upper, lower], axis=0) + one_three[2 * half :].astype(F32)
    two = along_z(two.astype(SENT), -2)
    loss = with_partner(loss, "z", 4)
    two, loss = tied(two, loss)
    two = two.astype(F32)
    given = row_half(one_three[: 2 * half], 1 - section).astype(F32) + row_half(two, 1 - section)
    got = lax.ppermute(given, "section", SWAP)
    loss = with_partner(with_partner(loss, "y", 1), "y", 2)
    mine = row_half(one_three[: 2 * half], section).astype(F32) + row_half(two, section)
    return kept[7 * half :] + mine + got, loss


def tower_kernel(spot, inputs, up, down, sent, own, ordered, up_held, down_held, sems):
    quarter = inputs.shape[0] // 4
    tensor = spot[0]
    step = STEP
    count = up.shape[1] // step
    loads = []
    for k, which in enumerate((1 - tensor, 3 - tensor, tensor, 2 + tensor)):
        start = pl.multiple_of(which * quarter, 16)
        rows = pl.ds(k * quarter, quarter)
        loads.append(
            pltpu.make_async_copy(
                inputs.at[pl.ds(start, quarter), :], ordered.at[rows, :], sems.at[k]
            )
        )
    for k in range(count):
        part = pl.ds(k * step, step)
        loads.append(
            pltpu.make_async_copy(up.at[:, part], up_held.at[:, part], sems.at[4 + 2 * k])
        )
        loads.append(
            pltpu.make_async_copy(down.at[part, :], down_held.at[part, :], sems.at[5 + 2 * k])
        )
    for load in loads:
        load.start()
    for load in loads[:4]:
        load.wait()
    total = jnp.zeros((4 * quarter, inputs.shape[1]), F32)
    hidden = None
    for k in range(count + 1):
        if k < count:
            loads[4 + 2 * k].wait()
        if k > 0:
            loads[3 + 2 * k].wait()
        if k < count:
            part = up_held[:, k * step : (k + 1) * step]
            coming = jnp.dot(ordered[...], part, preferred_element_type=F32)
        if k > 0:
            part = down_held[(k - 1) * step : k * step, :]
            total = total + jnp.dot(hidden, part, preferred_element_type=F32)
        if k < count:
            hidden = jax.nn.gelu(coming).astype(jnp.bfloat16)
    sent[...] = total[: 2 * quarter]
    own[...] = total[2 * quarter :] + ordered[2 * quarter :, :].astype(F32)


def tower(inputs, up, down, tensor):
    rows, width = inputs.shape
    units = up.shape[1]
    out = jax.ShapeDtypeStruct((rows // 2, width), F32)
    stays = pl.BlockSpec(memory_space=pltpu.HBM)
    sent, own = pl.pallas_call(
        tower_kernel,
        in_specs=[pl.BlockSpec(memory_space=pltpu.SMEM), stays, stays, stays],
        out_specs=[pl.BlockSpec(memory_space=pltpu.VMEM)] * 2,
        out_shape=[out, out],
        scratch_shapes=[
            pltpu.VMEM((rows, width), jnp.bfloat16),
            pltpu.VMEM((width, units), jnp.bfloat16),
            pltpu.VMEM((units, width), jnp.bfloat16),
            pltpu.SemaphoreType.DMA((4 + 2 * (units // STEP),)),
        ],
        compiler_params=pltpu.CompilerParams(vmem_limit_bytes=20 * 1024 * 1024),
        name="tower",
    )(
        jnp.reshape(tensor, (1,)).astype(jnp.int32),
        *(pltpu.with_memory_space_constraint(x, pltpu.HBM) for x in (inputs, up, down)),
    )
    raw = own + lax.ppermute(sent, "tensor", SWAP)
    norms = lax.rsqrt(jnp.sum(raw * raw, axis=-1, keepdims=True) + 1e-06)
    return (raw * norms).astype(jnp.bfloat16)


def pair_lanes(pair, tensor, quarter):
    rows = lax.dynamic_slice_in_dim(pair.reshape(2, 2, quarter), tensor, 1, 1)
    rows = rows.reshape(2 * quarter, 1)
    lane = lax.broadcasted_iota(jnp.int32, (2 * quarter, LANES), 1)
    digits = jnp.where(lane == 0, rows // LANES, jnp.where(lane == 1, rows % LANES, 0))
    return digits.astype(jnp.bfloat16)


def score_kernel(
    spot, scale, bias, own, one_three, two, four, one_three_other, two_other, four_other,
    reports, columns, kept, sent, report_part, loss, rows, weight, sems,
):
    count, width = reports.shape
    scale_value, bias_value = scale[0], bias[0]
    section = spot[0]
    quarter = own.shape[0] // 2
    place = 0
    groups = (
        (one_three, two, four, section),
        (one_three_other, two_other, four_other, 1 - section),
    )
    loads = []
    for group in groups:
        start = pl.multiple_of(group[3] * quarter, 16)
        for part in (*group[:3], own.at[pl.ds(start, quarter), :]):
            size = part.shape[0]
            held = rows.at[pl.ds(place, size), :]
            loads.append(pltpu.make_async_copy(part, held, sems.at[len(loads)]))
            place += size
    for load in loads:
        load.start()
    for load in loads:
        load.wait()

    total = jnp.zeros((1, count), F32)
    step = place // 4
    for k in range(4):
        start, stop = k * step, (k + 1) * step
        marks = rows[start:stop, width : width + 2].astype(F32)
        wanted = marks[:, 0:1] * LANES + marks[:, 1:2]
        dots = lax.dot_general(
            rows[start:stop, :width],
            reports[...],
            (((1,), (1,)), ((), ())),
            preferred_element_type=F32,
        )
        logits = scale_value * dots + bias_value
        match = wanted == columns[...]
        turned = jnp.where(match, -logits, logits)
        small = jnp.exp(-jnp.abs(turned))
        losses = jnp.maximum(turned, 0.0) + jnp.log1p(small)
        total = total + jnp.sum(losses, axis=0, keepdims=True)
        sigmoid = jnp.where(turned >= 0, 1.0, small) / (1.0 + small)
        signed = jnp.where(match, -scale_value, scale_value) * sigmoid
        weight[start:stop, :] = signed.astype(jnp.bfloat16)
    half = 2 * step
    loss[...] = jnp.broadcast_to(jnp.sum(total, axis=1, keepdims=True), loss.shape)
    kept[...] = weight[:half, :]
    sent[...] = jnp.dot(weight[half:, :], reports[...], preferred_element_type=F32)
    report_part[...] = transposed_dot(weight[...], rows[:, :width])


def scored(scale, bias, own, pieces, reports, columns):
    count, width = reports.shape
    rows = own.shape[0] + sum(piece.shape[0] for piece in pieces)
    spot = jnp.reshape(lax.axis_index("section"), (1,)).astype(jnp.int32)
    scalar = pl.BlockSpec(memory_space=pltpu.SMEM)
    whole = pl.BlockSpec(memory_space=pltpu.VMEM)
    return pl.pallas_call(
        score_kernel,
        in_specs=[scalar] * 3 + [pl.BlockSpec(memory_space=pltpu.HBM)] * 7 + [whole] * 2,
        out_specs=[whole, whole, whole, whole],
        out_shape=[
            jax.ShapeDtypeStruct((rows // 2, count), jnp.bfloat16),
            jax.ShapeDtypeStruct((rows // 2, width), F32),
            jax.ShapeDtypeStruct((count, width), F32),
            jax.ShapeDtypeStruct((1, LANES), F32),
        ],
        scratch_shapes=[
            pltpu.VMEM((rows, own.shape[1]), jnp.bfloat16),
            pltpu.VMEM((rows, count), jnp.bfloat16),
            pltpu.SemaphoreType.DMA((8,)),
        ],
        compiler_params=pltpu.CompilerParams(vmem_limit_bytes=12 * 1024 * 1024),
        name="scores",
    )(
        spot,
        scale,
        bias,
        *(pltpu.with_memory_space_constraint(x, pltpu.HBM) for x in (own, *pieces)),
        reports,
        columns,
    )


def transposed_dot(weight, slides):
    return lax.dot_general(weight, slides, (((0,), (0,)), ((), ())), preferred_element_type=F32)


def local(tower_input, up_weight, down_weight, pair, scale, bias):
    section = lax.axis_index("section")
    tensor = lax.axis_index("tensor")
    n_z = lax.axis_size("z")
    n_plane = lax.axis_size(PLANE)
    quarter, width = tower_input.shape[1] // 4, tower_input.shape[2]
    total = lax.axis_size(ALL) * quarter

    lanes = pair_lanes(pair, tensor, quarter)
    embedded = tower(tower_input[0], up_weight[0], down_weight[0], tensor)
    swapped = lax.ppermute(embedded, "section", SWAP)
    slides = jnp.concatenate([jnp.where(section == 0, embedded, swapped), lanes], axis=1)
    reports = row_half(jnp.where(section == 0, swapped, embedded), section)

    repeated = jnp.broadcast_to(reports, (n_plane, *reports.shape))
    repeated, slides = tied(repeated, slides)
    reports_all = exchanged(repeated, PLANE).reshape(n_plane * quarter, -1)
    pieces, reports_all = gathered_over_z(slides, section, reports_all)

    place = jnp.arange(n_plane * quarter, dtype=jnp.int32)
    member, row = place // quarter, place % quarter
    owner = ((member // 2 * n_z + lax.axis_index("z")) * 2 + section) * 2 + member % 2
    columns = (owner * quarter + row).astype(F32)

    weight, sent, report_part, loss = scored(
        scale, bias, slides, pieces, reports_all, columns[None, :]
    )
    back = lax.ppermute(sent, "section", SWAP)
    loss = with_partner(loss, "tensor", 1)
    report_part = report_part.astype(SENT).reshape(n_plane, quarter, width)
    report_part, loss = tied(report_part, loss)
    loss = with_partner(loss, "xl", 1)
    report_part, loss, weight = tied(report_part, loss, weight)
    report_terms = exchanged(report_part, PLANE)
    loss = with_partner(loss, "section", 1)
    back, loss = tied(back, loss)
    kept = jnp.dot(weight, reports_all, preferred_element_type=F32) + back
    slide_grad, loss = summed_over_z(kept, section, loss)
    report_grad = report_terms.astype(F32).sum(axis=0)
    return (loss[0, :1] / total, slide_grad, report_grad)


def solution(mesh):
    finer = Mesh(
        mesh.devices.reshape(2, 4, 8, mesh.shape["section"], mesh.shape["tensor"]),
        ALL,
    )
    return jax.shard_map(
        local,
        mesh=finer,
        in_specs=(
            P("section", DP, None),
            P("section", None, "tensor"),
            P("section", "tensor", None),
            P(DP),
            P(),
            P(),
        ),
        out_specs=(P(), P(ALL, None), P(ALL, None)),
        check_vma=False,
    )
```

```python
import jax
import jax.numpy as jnp
from jax import lax
from jax.sharding import Mesh
from jax.sharding import PartitionSpec as P
from jax.experimental import pallas as pl
from jax.experimental.pallas import tpu as pltpu

DP = ("xl", "y", "z")
PLANE = ("xl", "y", "tensor")
ALL = ("xl", "y", "z", "section", "tensor")
SWAP = [(0, 1), (1, 0)]
LANES = 128
STEP = 512
F32 = jnp.float32
SENT = jnp.float16


def exchanged(parts, axes):
    return lax.all_to_all(parts, axes, split_axis=0, concat_axis=0, tiled=True)


def copies(array, axes):
    return exchanged(jnp.broadcast_to(array, (lax.axis_size(axes), *array.shape)), axes)


def along_z(array, chips):
    n = lax.axis_size("z")
    pairs = []
    for z in range(n):
        pairs.append((2 * z, 2 * ((z + chips) % n)))
        pairs.append((2 * z + 1, 2 * ((z - chips) % n) + 1))
    return lax.ppermute(array, ("z", "section"), pairs)


def row_half(array, which):
    half = array.shape[0] // 2
    return lax.dynamic_slice_in_dim(array, which * half, half, 0)


def gathered_over_z(own, section, reports):
    two = along_z(own, 2)
    two_swapped = lax.ppermute(two, "section", SWAP)
    one_three = along_z(jnp.concatenate([own, two], axis=0), 1)
    four = along_z(row_half(two, section), 2)
    one_three, four = tied(one_three, four)
    others = [lax.ppermute(one_three, "section", SWAP), two_swapped]
    others.append(lax.ppermute(four, "section", SWAP))
    return [one_three, two, four, *others], reports


def tied(*arrays):
    return lax.optimization_barrier(arrays)


def with_partner(value, axis, bit):
    pairs = [(i, i ^ bit) for i in range(lax.axis_size(axis))]
    return value + lax.ppermute(value, axis, pairs)


def summed_over_z(kept, section, loss):
    half = kept.shape[0] // 8
    one_three = along_z(kept[: 4 * half].astype(SENT), -1)
    four = along_z(kept[6 * half : 7 * half].astype(SENT), -2)
    loss = with_partner(with_partner(loss, "z", 1), "z", 2)
    one_three, four, loss = tied(one_three, four, loss)
    four = four.astype(F32)
    upper = kept[4 * half : 5 * half] + jnp.where(section == 0, four, 0.0)
    lower = kept[5 * half : 6 * half] + jnp.where(section == 0, 0.0, four)
    two = jnp.concatenate([upper, lower], axis=0) + one_three[2 * half :].astype(F32)
    two = along_z(two.astype(SENT), -2)
    loss = with_partner(loss, "z", 4)
    two, loss = tied(two, loss)
    two = two.astype(F32)
    given = row_half(one_three[: 2 * half], 1 - section).astype(F32) + row_half(two, 1 - section)
    got = lax.ppermute(given, "section", SWAP)
    mine = row_half(one_three[: 2 * half], section).astype(F32) + row_half(two, section)
    return kept[7 * half :] + mine + got, loss


def tower_kernel(spot, inputs, up, down, sent, own, ordered, up_held, down_held, sems):
    quarter = inputs.shape[0] // 4
    tensor = spot[0]
    step = STEP
    count = up.shape[1] // step
    loads = []
    for k, which in enumerate((1 - tensor, 3 - tensor, tensor, 2 + tensor)):
        start = pl.multiple_of(which * quarter, 16)
        rows = pl.ds(k * quarter, quarter)
        loads.append(
            pltpu.make_async_copy(
                inputs.at[pl.ds(start, quarter), :], ordered.at[rows, :], sems.at[k]
            )
        )
    for k in range(count):
        part = pl.ds(k * step, step)
        loads.append(
            pltpu.make_async_copy(up.at[:, part], up_held.at[:, part], sems.at[4 + 2 * k])
        )
        loads.append(
            pltpu.make_async_copy(down.at[part, :], down_held.at[part, :], sems.at[5 + 2 * k])
        )
    for load in loads:
        load.start()
    for load in loads[:4]:
        load.wait()
    total = jnp.zeros((4 * quarter, inputs.shape[1]), F32)
    hidden = None
    for k in range(count + 1):
        if k < count:
            loads[4 + 2 * k].wait()
        if k > 0:
            loads[3 + 2 * k].wait()
        if k < count:
            part = up_held[:, k * step : (k + 1) * step]
            coming = jnp.dot(ordered[...], part, preferred_element_type=F32)
        if k > 0:
            part = down_held[(k - 1) * step : k * step, :]
            total = total + jnp.dot(hidden, part, preferred_element_type=F32)
        if k < count:
            hidden = jax.nn.gelu(coming).astype(jnp.bfloat16)
    sent[...] = total[: 2 * quarter]
    own[...] = total[2 * quarter :] + ordered[2 * quarter :, :].astype(F32)


def tower(inputs, up, down, tensor):
    rows, width = inputs.shape
    units = up.shape[1]
    out = jax.ShapeDtypeStruct((rows // 2, width), F32)
    stays = pl.BlockSpec(memory_space=pltpu.HBM)
    sent, own = pl.pallas_call(
        tower_kernel,
        in_specs=[pl.BlockSpec(memory_space=pltpu.SMEM), stays, stays, stays],
        out_specs=[pl.BlockSpec(memory_space=pltpu.VMEM)] * 2,
        out_shape=[out, out],
        scratch_shapes=[
            pltpu.VMEM((rows, width), jnp.bfloat16),
            pltpu.VMEM((width, units), jnp.bfloat16),
            pltpu.VMEM((units, width), jnp.bfloat16),
            pltpu.SemaphoreType.DMA((4 + 2 * (units // STEP),)),
        ],
        compiler_params=pltpu.CompilerParams(vmem_limit_bytes=20 * 1024 * 1024),
        name="tower",
    )(
        jnp.reshape(tensor, (1,)).astype(jnp.int32),
        *(pltpu.with_memory_space_constraint(x, pltpu.HBM) for x in (inputs, up, down)),
    )
    raw = own + lax.ppermute(sent, "tensor", SWAP)
    norms = lax.rsqrt(jnp.sum(raw * raw, axis=-1, keepdims=True) + 1e-06)
    return (raw * norms).astype(jnp.bfloat16)


def pair_lanes(pair, tensor, quarter):
    rows = lax.dynamic_slice_in_dim(pair.reshape(2, 2, quarter), tensor, 1, 1)
    rows = rows.reshape(2 * quarter, 1)
    lane = lax.broadcasted_iota(jnp.int32, (2 * quarter, LANES), 1)
    digits = jnp.where(lane == 0, rows // LANES, jnp.where(lane == 1, rows % LANES, 0))
    return digits.astype(jnp.bfloat16)


def score_kernel(
    spot, scale, bias, own, one_three, two, four, one_three_other, two_other, four_other,
    reports, columns, kept, sent, report_part, loss, rows, weight, sems,
):
    count, width = reports.shape
    scale_value, bias_value = scale[0], bias[0]
    section = spot[0]
    quarter = own.shape[0] // 2
    place = 0
    groups = (
        (one_three, two, four, section),
        (one_three_other, two_other, four_other, 1 - section),
    )
    loads = []
    for group in groups:
        start = pl.multiple_of(group[3] * quarter, 16)
        for part in (*group[:3], own.at[pl.ds(start, quarter), :]):
            size = part.shape[0]
            held = rows.at[pl.ds(place, size), :]
            loads.append(pltpu.make_async_copy(part, held, sems.at[len(loads)]))
            place += size
    for load in loads:
        load.start()
    needed = (loads[:1], loads[1:4], loads[4:5], loads[5:])

    total = jnp.zeros((1, count), F32)
    step = place // 4
    for k in range(4):
        start, stop = k * step, (k + 1) * step
        for load in needed[k]:
            load.wait()
        marks = rows[start:stop, width : width + 2].astype(F32)
        wanted = marks[:, 0:1] * LANES + marks[:, 1:2]
        dots = lax.dot_general(
            rows[start:stop, :width],
            reports[...],
            (((1,), (1,)), ((), ())),
            preferred_element_type=F32,
        )
        logits = scale_value * dots + bias_value
        match = wanted == columns[...]
        turned = jnp.where(match, -logits, logits)
        small = jnp.exp(-jnp.abs(turned))
        losses = jnp.maximum(turned, 0.0) + jnp.log1p(small)
        total = total + jnp.sum(losses, axis=0, keepdims=True)
        sigmoid = jnp.where(turned >= 0, 1.0, small) / (1.0 + small)
        signed = jnp.where(match, -scale_value, scale_value) * sigmoid
        weight[start:stop, :] = signed.astype(jnp.bfloat16)
    half = 2 * step
    loss[...] = jnp.broadcast_to(jnp.sum(total, axis=1, keepdims=True), loss.shape)
    kept[...] = weight[:half, :]
    sent[...] = jnp.dot(weight[half:, :], reports[...], preferred_element_type=F32)
    report_part[...] = transposed_dot(weight[...], rows[:, :width])


def scored(scale, bias, own, pieces, reports, columns):
    count, width = reports.shape
    rows = own.shape[0] + sum(piece.shape[0] for piece in pieces)
    spot = jnp.reshape(lax.axis_index("section"), (1,)).astype(jnp.int32)
    scalar = pl.BlockSpec(memory_space=pltpu.SMEM)
    whole = pl.BlockSpec(memory_space=pltpu.VMEM)
    return pl.pallas_call(
        score_kernel,
        in_specs=[scalar] * 3 + [pl.BlockSpec(memory_space=pltpu.HBM)] * 7 + [whole] * 2,
        out_specs=[whole, whole, whole, whole],
        out_shape=[
            jax.ShapeDtypeStruct((rows // 2, count), jnp.bfloat16),
            jax.ShapeDtypeStruct((rows // 2, width), F32),
            jax.ShapeDtypeStruct((count, width), F32),
            jax.ShapeDtypeStruct((1, LANES), F32),
        ],
        scratch_shapes=[
            pltpu.VMEM((rows, own.shape[1]), jnp.bfloat16),
            pltpu.VMEM((rows, count), jnp.bfloat16),
            pltpu.SemaphoreType.DMA((8,)),
        ],
        compiler_params=pltpu.CompilerParams(vmem_limit_bytes=12 * 1024 * 1024),
        name="scores",
    )(
        spot,
        scale,
        bias,
        *(pltpu.with_memory_space_constraint(x, pltpu.HBM) for x in (own, *pieces)),
        reports,
        columns,
    )


def transposed_dot(weight, slides):
    return lax.dot_general(weight, slides, (((0,), (0,)), ((), ())), preferred_element_type=F32)


def local(tower_input, up_weight, down_weight, pair, scale, bias):
    section = lax.axis_index("section")
    tensor = lax.axis_index("tensor")
    n_z = lax.axis_size("z")
    n_plane = lax.axis_size(PLANE)
    quarter, width = tower_input.shape[1] // 4, tower_input.shape[2]
    total = lax.axis_size(ALL) * quarter

    lanes = pair_lanes(pair, tensor, quarter)
    embedded = tower(tower_input[0], up_weight[0], down_weight[0], tensor)
    swapped = lax.ppermute(embedded, "section", SWAP)
    slides = jnp.concatenate([jnp.where(section == 0, embedded, swapped), lanes], axis=1)
    reports = row_half(jnp.where(section == 0, swapped, embedded), section)

    repeated = jnp.broadcast_to(reports, (n_plane, *reports.shape))
    repeated, slides = tied(repeated, slides)
    reports_all = exchanged(repeated, PLANE).reshape(n_plane * quarter, -1)
    pieces, reports_all = gathered_over_z(slides, section, reports_all)

    place = jnp.arange(n_plane * quarter, dtype=jnp.int32)
    member, row = place // quarter, place % quarter
    owner = ((member // 2 * n_z + lax.axis_index("z")) * 2 + section) * 2 + member % 2
    columns = (owner * quarter + row).astype(F32)

    weight, sent, report_part, loss = scored(
        scale, bias, slides, pieces, reports_all, columns[None, :]
    )
    back = lax.ppermute(sent, "section", SWAP)
    report_part = report_part.astype(SENT).reshape(n_plane, quarter, width)
    report_part, weight = tied(report_part, weight)
    report_terms = exchanged(report_part, PLANE)
    loss = with_partner(loss, "section", 1)
    back, loss = tied(back, loss)
    kept = jnp.dot(weight, reports_all, preferred_element_type=F32) + back
    slide_grad, loss = summed_over_z(kept, section, loss)
    report_terms, loss = tied(report_terms, loss)
    report_grad = report_terms.astype(F32).sum(axis=0)
    loss, report_grad = tied(with_partner(loss, "tensor", 1), report_grad)
    loss, slide_grad = tied(with_partner(loss, "xl", 1), slide_grad)
    loss = with_partner(with_partner(loss, "y", 1), "y", 2)
    return (loss[0, :1] / total, slide_grad, report_grad)


def solution(mesh):
    finer = Mesh(
        mesh.devices.reshape(2, 4, 8, mesh.shape["section"], mesh.shape["tensor"]),
        ALL,
    )
    return jax.shard_map(
        local,
        mesh=finer,
        in_specs=(
            P("section", DP, None),
            P("section", None, "tensor"),
            P("section", "tensor", None),
            P(DP),
            P(),
            P(),
        ),
        out_specs=(P(), P(ALL, None), P(ALL, None)),
        check_vma=False,
    )
```

```python
import jax
import jax.numpy as jnp
from jax import lax
from jax.sharding import Mesh
from jax.sharding import PartitionSpec as P
from jax.experimental import pallas as pl
from jax.experimental.pallas import tpu as pltpu

DP = ("xl", "y", "z")
PLANE = ("xl", "y", "tensor")
ALL = ("xl", "y", "z", "section", "tensor")
SWAP = [(0, 1), (1, 0)]
LANES = 128
STEP = 512
F32 = jnp.float32
SENT = jnp.float16


def exchanged(parts, axes):
    return lax.all_to_all(parts, axes, split_axis=0, concat_axis=0, tiled=True)


def copies(array, axes):
    return exchanged(jnp.broadcast_to(array, (lax.axis_size(axes), *array.shape)), axes)


def along_z(array, chips):
    n = lax.axis_size("z")
    pairs = []
    for z in range(n):
        pairs.append((2 * z, 2 * ((z + chips) % n)))
        pairs.append((2 * z + 1, 2 * ((z - chips) % n) + 1))
    return lax.ppermute(array, ("z", "section"), pairs)


def row_half(array, which):
    half = array.shape[0] // 2
    return lax.dynamic_slice_in_dim(array, which * half, half, 0)


def gathered_over_z(own, section):
    two = along_z(own, 2)
    one = along_z(own, 1)
    one, two = tied(one, two)
    three = along_z(two, 1)
    four = along_z(row_half(two, section), 2)
    early = [lax.ppermute(piece, "section", SWAP) for piece in (one, two)]
    three, four = tied(three, four)
    late = [lax.ppermute(piece, "section", SWAP) for piece in (three, four)]
    return [one, three, two, four, early[0], late[0], early[1], late[1]]


def tied(*arrays):
    return lax.optimization_barrier(arrays)


def with_partner(value, axis, bit):
    pairs = [(i, i ^ bit) for i in range(lax.axis_size(axis))]
    return value + lax.ppermute(value, axis, pairs)


def summed_over_z(kept, section, loss):
    half = kept.shape[0] // 8
    one_three = along_z(kept[: 4 * half].astype(SENT), -1)
    four = along_z(kept[6 * half : 7 * half].astype(SENT), -2)
    loss = with_partner(with_partner(loss, "z", 1), "z", 2)
    one_three, four, loss = tied(one_three, four, loss)
    four = four.astype(F32)
    upper = kept[4 * half : 5 * half] + jnp.where(section == 0, four, 0.0)
    lower = kept[5 * half : 6 * half] + jnp.where(section == 0, 0.0, four)
    two = jnp.concatenate([upper, lower], axis=0) + one_three[2 * half :].astype(F32)
    two = along_z(two.astype(SENT), -2)
    loss = with_partner(loss, "z", 4)
    two, loss = tied(two, loss)
    two = two.astype(F32)
    given = row_half(one_three[: 2 * half], 1 - section).astype(F32) + row_half(two, 1 - section)
    got = lax.ppermute(given, "section", SWAP)
    mine = row_half(one_three[: 2 * half], section).astype(F32) + row_half(two, section)
    return kept[7 * half :] + mine + got, loss


def tower_kernel(spot, inputs, up, down, sent, own, ordered, up_held, down_held, sems):
    quarter = inputs.shape[0] // 4
    tensor = spot[0]
    step = STEP
    count = up.shape[1] // step
    loads = []
    for k, which in enumerate((1 - tensor, 3 - tensor, tensor, 2 + tensor)):
        start = pl.multiple_of(which * quarter, 16)
        rows = pl.ds(k * quarter, quarter)
        loads.append(
            pltpu.make_async_copy(
                inputs.at[pl.ds(start, quarter), :], ordered.at[rows, :], sems.at[k]
            )
        )
    for k in range(count):
        part = pl.ds(k * step, step)
        loads.append(
            pltpu.make_async_copy(up.at[:, part], up_held.at[:, part], sems.at[4 + 2 * k])
        )
        loads.append(
            pltpu.make_async_copy(down.at[part, :], down_held.at[part, :], sems.at[5 + 2 * k])
        )
    for load in loads:
        load.start()
    for load in loads[:4]:
        load.wait()
    total = jnp.zeros((4 * quarter, inputs.shape[1]), F32)
    hidden = None
    for k in range(count + 1):
        if k < count:
            loads[4 + 2 * k].wait()
        if k > 0:
            loads[3 + 2 * k].wait()
        if k < count:
            part = up_held[:, k * step : (k + 1) * step]
            coming = jnp.dot(ordered[...], part, preferred_element_type=F32)
        if k > 0:
            part = down_held[(k - 1) * step : k * step, :]
            total = total + jnp.dot(hidden, part, preferred_element_type=F32)
        if k < count:
            hidden = jax.nn.gelu(coming).astype(jnp.bfloat16)
    sent[...] = total[: 2 * quarter]
    own[...] = total[2 * quarter :] + ordered[2 * quarter :, :].astype(F32)


def tower(inputs, up, down, tensor):
    rows, width = inputs.shape
    units = up.shape[1]
    out = jax.ShapeDtypeStruct((rows // 2, width), F32)
    stays = pl.BlockSpec(memory_space=pltpu.HBM)
    sent, own = pl.pallas_call(
        tower_kernel,
        in_specs=[pl.BlockSpec(memory_space=pltpu.SMEM), stays, stays, stays],
        out_specs=[pl.BlockSpec(memory_space=pltpu.VMEM)] * 2,
        out_shape=[out, out],
        scratch_shapes=[
            pltpu.VMEM((rows, width), jnp.bfloat16),
            pltpu.VMEM((width, units), jnp.bfloat16),
            pltpu.VMEM((units, width), jnp.bfloat16),
            pltpu.SemaphoreType.DMA((4 + 2 * (units // STEP),)),
        ],
        compiler_params=pltpu.CompilerParams(vmem_limit_bytes=20 * 1024 * 1024),
        name="tower",
    )(
        jnp.reshape(tensor, (1,)).astype(jnp.int32),
        *(pltpu.with_memory_space_constraint(x, pltpu.HBM) for x in (inputs, up, down)),
    )
    raw = own + lax.ppermute(sent, "tensor", SWAP)
    norms = lax.rsqrt(jnp.sum(raw * raw, axis=-1, keepdims=True) + 1e-06)
    return (raw * norms).astype(jnp.bfloat16)


def pair_lanes(pair, tensor, quarter):
    rows = lax.dynamic_slice_in_dim(pair.reshape(2, 2, quarter), tensor, 1, 1)
    rows = rows.reshape(2 * quarter, 1)
    lane = lax.broadcasted_iota(jnp.int32, (2 * quarter, LANES), 1)
    digits = jnp.where(lane == 0, rows // LANES, jnp.where(lane == 1, rows % LANES, 0))
    return digits.astype(jnp.bfloat16)


def score_kernel(
    spot, scale, bias, own, one, three, two, four, one_other, three_other, two_other,
    four_other, reports, columns, kept, sent, report_part, loss, rows, weight, sems,
):
    count, width = reports.shape
    scale_value, bias_value = scale[0], bias[0]
    section = spot[0]
    quarter = own.shape[0] // 2
    place = 0
    groups = (
        (one, three, two, four, section),
        (one_other, three_other, two_other, four_other, 1 - section),
    )
    loads = []
    for group in groups:
        start = pl.multiple_of(group[4] * quarter, 16)
        for part in (*group[:4], own.at[pl.ds(start, quarter), :]):
            size = part.shape[0]
            held = rows.at[pl.ds(place, size), :]
            loads.append(pltpu.make_async_copy(part, held, sems.at[len(loads)]))
            place += size
    for load in loads:
        load.start()
    for load in loads:
        load.wait()

    total = jnp.zeros((1, count), F32)
    step = place // 4
    for k in range(4):
        start, stop = k * step, (k + 1) * step
        marks = rows[start:stop, width : width + 2].astype(F32)
        wanted = marks[:, 0:1] * LANES + marks[:, 1:2]
        dots = lax.dot_general(
            rows[start:stop, :width],
            reports[...],
            (((1,), (1,)), ((), ())),
            preferred_element_type=F32,
        )
        logits = scale_value * dots + bias_value
        match = wanted == columns[...]
        turned = jnp.where(match, -logits, logits)
        small = jnp.exp(-jnp.abs(turned))
        losses = jnp.maximum(turned, 0.0) + jnp.log1p(small)
        total = total + jnp.sum(losses, axis=0, keepdims=True)
        sigmoid = jnp.where(turned >= 0, 1.0, small) / (1.0 + small)
        signed = jnp.where(match, -scale_value, scale_value) * sigmoid
        weight[start:stop, :] = signed.astype(jnp.bfloat16)
    half = 2 * step
    loss[...] = jnp.broadcast_to(jnp.sum(total, axis=1, keepdims=True), loss.shape)
    kept[...] = weight[:half, :]
    sent[...] = jnp.dot(weight[half:, :], reports[...], preferred_element_type=F32)
    report_part[...] = transposed_dot(weight[...], rows[:, :width])


def scored(scale, bias, own, pieces, reports, columns):
    count, width = reports.shape
    rows = own.shape[0] + sum(piece.shape[0] for piece in pieces)
    spot = jnp.reshape(lax.axis_index("section"), (1,)).astype(jnp.int32)
    scalar = pl.BlockSpec(memory_space=pltpu.SMEM)
    whole = pl.BlockSpec(memory_space=pltpu.VMEM)
    return pl.pallas_call(
        score_kernel,
        in_specs=[scalar] * 3 + [pl.BlockSpec(memory_space=pltpu.HBM)] * 9 + [whole] * 2,
        out_specs=[whole, whole, whole, whole],
        out_shape=[
            jax.ShapeDtypeStruct((rows // 2, count), jnp.bfloat16),
            jax.ShapeDtypeStruct((rows // 2, width), F32),
            jax.ShapeDtypeStruct((count, width), F32),
            jax.ShapeDtypeStruct((1, LANES), F32),
        ],
        scratch_shapes=[
            pltpu.VMEM((rows, own.shape[1]), jnp.bfloat16),
            pltpu.VMEM((rows, count), jnp.bfloat16),
            pltpu.SemaphoreType.DMA((10,)),
        ],
        compiler_params=pltpu.CompilerParams(vmem_limit_bytes=12 * 1024 * 1024),
        name="scores",
    )(
        spot,
        scale,
        bias,
        *(pltpu.with_memory_space_constraint(x, pltpu.HBM) for x in (own, *pieces)),
        reports,
        columns,
    )


def transposed_dot(weight, slides):
    return lax.dot_general(weight, slides, (((0,), (0,)), ((), ())), preferred_element_type=F32)


def local(tower_input, up_weight, down_weight, pair, scale, bias):
    section = lax.axis_index("section")
    tensor = lax.axis_index("tensor")
    n_z = lax.axis_size("z")
    n_plane = lax.axis_size(PLANE)
    quarter, width = tower_input.shape[1] // 4, tower_input.shape[2]
    total = lax.axis_size(ALL) * quarter

    lanes = pair_lanes(pair, tensor, quarter)
    embedded = tower(tower_input[0], up_weight[0], down_weight[0], tensor)
    swapped = lax.ppermute(embedded, "section", SWAP)
    slides = jnp.concatenate([jnp.where(section == 0, embedded, swapped), lanes], axis=1)
    reports = row_half(jnp.where(section == 0, swapped, embedded), section)

    repeated = jnp.broadcast_to(reports, (n_plane, *reports.shape))
    repeated, slides = tied(repeated, slides)
    reports_all = exchanged(repeated, PLANE).reshape(n_plane * quarter, -1)
    pieces = gathered_over_z(slides, section)

    place = jnp.arange(n_plane * quarter, dtype=jnp.int32)
    member, row = place // quarter, place % quarter
    owner = ((member // 2 * n_z + lax.axis_index("z")) * 2 + section) * 2 + member % 2
    columns = (owner * quarter + row).astype(F32)

    weight, sent, report_part, loss = scored(
        scale, bias, slides, pieces, reports_all, columns[None, :]
    )
    back = lax.ppermute(sent, "section", SWAP)
    loss = with_partner(loss, "tensor", 1)
    report_part = report_part.astype(SENT).reshape(n_plane, quarter, width)
    report_part, loss = tied(report_part, loss)
    loss = with_partner(loss, "xl", 1)
    report_part, loss, weight = tied(report_part, loss, weight)
    report_terms = exchanged(report_part, PLANE)
    loss = with_partner(loss, "section", 1)
    back, loss = tied(back, loss)
    kept = jnp.dot(weight, reports_all, preferred_element_type=F32) + back
    slide_grad, loss = summed_over_z(kept, section, loss)
    report_terms, loss = tied(report_terms, loss)
    report_grad = report_terms.astype(F32).sum(axis=0)
    loss, report_grad = tied(with_partner(loss, "y", 1), report_grad)
    loss = with_partner(loss, "y", 2)
    return (loss[0, :1] / total, slide_grad, report_grad)


def solution(mesh):
    finer = Mesh(
        mesh.devices.reshape(2, 4, 8, mesh.shape["section"], mesh.shape["tensor"]),
        ALL,
    )
    return jax.shard_map(
        local,
        mesh=finer,
        in_specs=(
            P("section", DP, None),
            P("section", None, "tensor"),
            P("section", "tensor", None),
            P(DP),
            P(),
            P(),
        ),
        out_specs=(P(), P(ALL, None), P(ALL, None)),
        check_vma=False,
    )
```

```python
import jax
import jax.numpy as jnp
from jax import lax
from jax.sharding import Mesh
from jax.sharding import PartitionSpec as P
from jax.experimental import pallas as pl
from jax.experimental.pallas import tpu as pltpu

DP = ("xl", "y", "z")
PLANE = ("xl", "y", "tensor")
ALL = ("xl", "y", "z", "section", "tensor")
SWAP = [(0, 1), (1, 0)]
LANES = 128
STEP = 512
F32 = jnp.float32
SENT = jnp.float16


def exchanged(parts, axes):
    return lax.all_to_all(parts, axes, split_axis=0, concat_axis=0, tiled=True)


def copies(array, axes):
    return exchanged(jnp.broadcast_to(array, (lax.axis_size(axes), *array.shape)), axes)


def along_z(array, chips):
    n = lax.axis_size("z")
    pairs = []
    for z in range(n):
        pairs.append((2 * z, 2 * ((z + chips) % n)))
        pairs.append((2 * z + 1, 2 * ((z - chips) % n) + 1))
    return lax.ppermute(array, ("z", "section"), pairs)


def row_half(array, which):
    half = array.shape[0] // 2
    return lax.dynamic_slice_in_dim(array, which * half, half, 0)


def gathered_over_z(own, section):
    two = along_z(own, 2)
    one = along_z(own, 1)
    one, two = tied(one, two)
    three = along_z(two, 1)
    four = along_z(row_half(two, section), 2)
    early = [lax.ppermute(piece, "section", SWAP) for piece in (one, two)]
    three, four = tied(three, four)
    late = [lax.ppermute(piece, "section", SWAP) for piece in (three, four)]
    return [one, three, two, four, early[0], late[0], early[1], late[1]]


def tied(*arrays):
    return lax.optimization_barrier(arrays)


def with_partner(value, axis, bit):
    pairs = [(i, i ^ bit) for i in range(lax.axis_size(axis))]
    return value + lax.ppermute(value, axis, pairs)


def with_other_three(value, axes):
    first, second, third = (
        lax.ppermute(value, axes, [(i, i ^ k) for i in range(4)]) for k in (1, 2, 3)
    )
    return (value + first) + (second + third)


def summed_over_z(kept, section, loss):
    half = kept.shape[0] // 8
    one_three = along_z(kept[: 4 * half].astype(SENT), -1)
    four = along_z(kept[6 * half : 7 * half].astype(SENT), -2)
    loss = with_partner(with_partner(loss, "z", 1), "z", 2)
    one_three, four, loss = tied(one_three, four, loss)
    four = four.astype(F32)
    upper = kept[4 * half : 5 * half] + jnp.where(section == 0, four, 0.0)
    lower = kept[5 * half : 6 * half] + jnp.where(section == 0, 0.0, four)
    two = jnp.concatenate([upper, lower], axis=0) + one_three[2 * half :].astype(F32)
    two = along_z(two.astype(SENT), -2)
    loss = with_partner(loss, "z", 4)
    two, loss = tied(two, loss)
    two = two.astype(F32)
    given = row_half(one_three[: 2 * half], 1 - section).astype(F32) + row_half(two, 1 - section)
    got = lax.ppermute(given, "section", SWAP)
    mine = row_half(one_three[: 2 * half], section).astype(F32) + row_half(two, section)
    return kept[7 * half :] + mine + got, loss


def tower_kernel(spot, inputs, up, down, sent, own, ordered, up_held, down_held, sems):
    quarter = inputs.shape[0] // 4
    tensor = spot[0]
    step = STEP
    count = up.shape[1] // step
    loads = []
    for k, which in enumerate((1 - tensor, 3 - tensor, tensor, 2 + tensor)):
        start = pl.multiple_of(which * quarter, 16)
        rows = pl.ds(k * quarter, quarter)
        loads.append(
            pltpu.make_async_copy(
                inputs.at[pl.ds(start, quarter), :], ordered.at[rows, :], sems.at[k]
            )
        )
    for k in range(count):
        part = pl.ds(k * step, step)
        loads.append(
            pltpu.make_async_copy(up.at[:, part], up_held.at[:, part], sems.at[4 + 2 * k])
        )
        loads.append(
            pltpu.make_async_copy(down.at[part, :], down_held.at[part, :], sems.at[5 + 2 * k])
        )
    for load in loads:
        load.start()
    for load in loads[:4]:
        load.wait()
    total = jnp.zeros((4 * quarter, inputs.shape[1]), F32)
    hidden = None
    for k in range(count + 1):
        if k < count:
            loads[4 + 2 * k].wait()
        if k > 0:
            loads[3 + 2 * k].wait()
        if k < count:
            part = up_held[:, k * step : (k + 1) * step]
            coming = jnp.dot(ordered[...], part, preferred_element_type=F32)
        if k > 0:
            part = down_held[(k - 1) * step : k * step, :]
            total = total + jnp.dot(hidden, part, preferred_element_type=F32)
        if k < count:
            hidden = jax.nn.gelu(coming).astype(jnp.bfloat16)
    sent[...] = total[: 2 * quarter]
    own[...] = total[2 * quarter :] + ordered[2 * quarter :, :].astype(F32)


def tower(inputs, up, down, tensor):
    rows, width = inputs.shape
    units = up.shape[1]
    out = jax.ShapeDtypeStruct((rows // 2, width), F32)
    stays = pl.BlockSpec(memory_space=pltpu.HBM)
    sent, own = pl.pallas_call(
        tower_kernel,
        in_specs=[pl.BlockSpec(memory_space=pltpu.SMEM), stays, stays, stays],
        out_specs=[pl.BlockSpec(memory_space=pltpu.VMEM)] * 2,
        out_shape=[out, out],
        scratch_shapes=[
            pltpu.VMEM((rows, width), jnp.bfloat16),
            pltpu.VMEM((width, units), jnp.bfloat16),
            pltpu.VMEM((units, width), jnp.bfloat16),
            pltpu.SemaphoreType.DMA((4 + 2 * (units // STEP),)),
        ],
        compiler_params=pltpu.CompilerParams(vmem_limit_bytes=20 * 1024 * 1024),
        name="tower",
    )(
        jnp.reshape(tensor, (1,)).astype(jnp.int32),
        *(pltpu.with_memory_space_constraint(x, pltpu.HBM) for x in (inputs, up, down)),
    )
    raw = own + lax.ppermute(sent, "tensor", SWAP)
    norms = lax.rsqrt(jnp.sum(raw * raw, axis=-1, keepdims=True) + 1e-06)
    return (raw * norms).astype(jnp.bfloat16)


def pair_lanes(pair, tensor, quarter):
    rows = lax.dynamic_slice_in_dim(pair.reshape(2, 2, quarter), tensor, 1, 1)
    rows = rows.reshape(2 * quarter, 1)
    lane = lax.broadcasted_iota(jnp.int32, (2 * quarter, LANES), 1)
    digits = jnp.where(lane == 0, rows // LANES, jnp.where(lane == 1, rows % LANES, 0))
    return digits.astype(jnp.bfloat16)


def score_kernel(
    spot, scale, bias, own, one, three, two, four, one_other, three_other, two_other,
    four_other, reports, columns, kept, sent, report_part, loss, rows, weight, sems,
):
    count, width = reports.shape
    scale_value, bias_value = scale[0], bias[0]
    section = spot[0]
    quarter = own.shape[0] // 2
    place = 0
    groups = (
        (one, three, two, four, section),
        (one_other, three_other, two_other, four_other, 1 - section),
    )
    loads = []
    for group in groups:
        start = pl.multiple_of(group[4] * quarter, 16)
        for part in (*group[:4], own.at[pl.ds(start, quarter), :]):
            size = part.shape[0]
            held = rows.at[pl.ds(place, size), :]
            loads.append(pltpu.make_async_copy(part, held, sems.at[len(loads)]))
            place += size
    for load in loads:
        load.start()
    for load in loads:
        load.wait()

    total = jnp.zeros((1, count), F32)
    step = place // 4
    for k in range(4):
        start, stop = k * step, (k + 1) * step
        marks = rows[start:stop, width : width + 2].astype(F32)
        wanted = marks[:, 0:1] * LANES + marks[:, 1:2]
        dots = lax.dot_general(
            rows[start:stop, :width],
            reports[...],
            (((1,), (1,)), ((), ())),
            preferred_element_type=F32,
        )
        logits = scale_value * dots + bias_value
        match = wanted == columns[...]
        turned = jnp.where(match, -logits, logits)
        small = jnp.exp(-jnp.abs(turned))
        losses = jnp.maximum(turned, 0.0) + jnp.log1p(small)
        total = total + jnp.sum(losses, axis=0, keepdims=True)
        sigmoid = jnp.where(turned >= 0, 1.0, small) / (1.0 + small)
        signed = jnp.where(match, -scale_value, scale_value) * sigmoid
        weight[start:stop, :] = signed.astype(jnp.bfloat16)
    half = 2 * step
    loss[...] = jnp.broadcast_to(jnp.sum(total, axis=1, keepdims=True), loss.shape)
    kept[...] = weight[:half, :]
    sent[...] = jnp.dot(weight[half:, :], reports[...], preferred_element_type=F32)
    report_part[...] = transposed_dot(weight[...], rows[:, :width])


def scored(scale, bias, own, pieces, reports, columns):
    count, width = reports.shape
    rows = own.shape[0] + sum(piece.shape[0] for piece in pieces)
    spot = jnp.reshape(lax.axis_index("section"), (1,)).astype(jnp.int32)
    scalar = pl.BlockSpec(memory_space=pltpu.SMEM)
    whole = pl.BlockSpec(memory_space=pltpu.VMEM)
    return pl.pallas_call(
        score_kernel,
        in_specs=[scalar] * 3 + [pl.BlockSpec(memory_space=pltpu.HBM)] * 9 + [whole] * 2,
        out_specs=[whole, whole, whole, whole],
        out_shape=[
            jax.ShapeDtypeStruct((rows // 2, count), jnp.bfloat16),
            jax.ShapeDtypeStruct((rows // 2, width), F32),
            jax.ShapeDtypeStruct((count, width), F32),
            jax.ShapeDtypeStruct((1, LANES), F32),
        ],
        scratch_shapes=[
            pltpu.VMEM((rows, own.shape[1]), jnp.bfloat16),
            pltpu.VMEM((rows, count), jnp.bfloat16),
            pltpu.SemaphoreType.DMA((10,)),
        ],
        compiler_params=pltpu.CompilerParams(vmem_limit_bytes=12 * 1024 * 1024),
        name="scores",
    )(
        spot,
        scale,
        bias,
        *(pltpu.with_memory_space_constraint(x, pltpu.HBM) for x in (own, *pieces)),
        reports,
        columns,
    )


def transposed_dot(weight, slides):
    return lax.dot_general(weight, slides, (((0,), (0,)), ((), ())), preferred_element_type=F32)


def local(tower_input, up_weight, down_weight, pair, scale, bias):
    section = lax.axis_index("section")
    tensor = lax.axis_index("tensor")
    n_z = lax.axis_size("z")
    n_plane = lax.axis_size(PLANE)
    quarter, width = tower_input.shape[1] // 4, tower_input.shape[2]
    total = lax.axis_size(ALL) * quarter

    lanes = pair_lanes(pair, tensor, quarter)
    embedded = tower(tower_input[0], up_weight[0], down_weight[0], tensor)
    swapped = lax.ppermute(embedded, "section", SWAP)
    slides = jnp.concatenate([jnp.where(section == 0, embedded, swapped), lanes], axis=1)
    reports = row_half(jnp.where(section == 0, swapped, embedded), section)

    repeated = jnp.broadcast_to(reports, (n_plane, *reports.shape))
    repeated, slides = tied(repeated, slides)
    reports_all = exchanged(repeated, PLANE).reshape(n_plane * quarter, -1)
    pieces = gathered_over_z(slides, section)

    place = jnp.arange(n_plane * quarter, dtype=jnp.int32)
    member, row = place // quarter, place % quarter
    owner = ((member // 2 * n_z + lax.axis_index("z")) * 2 + section) * 2 + member % 2
    columns = (owner * quarter + row).astype(F32)

    weight, sent, report_part, loss = scored(
        scale, bias, slides, pieces, reports_all, columns[None, :]
    )
    back = lax.ppermute(sent, "section", SWAP)
    loss = with_other_three(loss, ("xl", "tensor"))
    report_part = report_part.astype(SENT).reshape(n_plane, quarter, width)
    report_part, loss, weight = tied(report_part, loss, weight)
    report_terms = exchanged(report_part, PLANE)
    loss = with_partner(loss, "section", 1)
    back, loss = tied(back, loss)
    kept = jnp.dot(weight, reports_all, preferred_element_type=F32) + back
    slide_grad, loss = summed_over_z(kept, section, loss)
    report_terms, loss = tied(report_terms, loss)
    report_grad = report_terms.astype(F32).sum(axis=0)
    loss, report_grad = tied(with_other_three(loss, "y"), report_grad)
    return (loss[0, :1] / total, slide_grad, report_grad)


def solution(mesh):
    finer = Mesh(
        mesh.devices.reshape(2, 4, 8, mesh.shape["section"], mesh.shape["tensor"]),
        ALL,
    )
    return jax.shard_map(
        local,
        mesh=finer,
        in_specs=(
            P("section", DP, None),
            P("section", None, "tensor"),
            P("section", "tensor", None),
            P(DP),
            P(),
            P(),
        ),
        out_specs=(P(), P(ALL, None), P(ALL, None)),
        check_vma=False,
    )
```

```python
import jax
import jax.numpy as jnp
from jax import lax
from jax.sharding import Mesh
from jax.sharding import PartitionSpec as P
from jax.experimental import pallas as pl
from jax.experimental.pallas import tpu as pltpu

DP = ("xl", "y", "z")
PLANE = ("xl", "y", "tensor")
ALL = ("xl", "y", "z", "section", "tensor")
SWAP = [(0, 1), (1, 0)]
LANES = 128
STEP = 512
F32 = jnp.float32
SENT = jnp.float16


def exchanged(parts, axes):
    return lax.all_to_all(parts, axes, split_axis=0, concat_axis=0, tiled=True)


def copies(array, axes):
    return exchanged(jnp.broadcast_to(array, (lax.axis_size(axes), *array.shape)), axes)


def along_z(array, chips):
    n = lax.axis_size("z")
    pairs = []
    for z in range(n):
        pairs.append((2 * z, 2 * ((z + chips) % n)))
        pairs.append((2 * z + 1, 2 * ((z - chips) % n) + 1))
    return lax.ppermute(array, ("z", "section"), pairs)


def row_half(array, which):
    half = array.shape[0] // 2
    return lax.dynamic_slice_in_dim(array, which * half, half, 0)


def gathered_over_z(own, section):
    two = along_z(own, 2)
    one = along_z(own, 1)
    one, two = tied(one, two)
    three = along_z(two, 1)
    four = along_z(row_half(two, section), 2)
    early = [lax.ppermute(piece, "section", SWAP) for piece in (one, two)]
    three, four = tied(three, four)
    late = [lax.ppermute(piece, "section", SWAP) for piece in (three, four)]
    return [one, three, two, four, early[0], late[0], early[1], late[1]]


def tied(*arrays):
    return lax.optimization_barrier(arrays)


def with_partner(value, axis, bit):
    pairs = [(i, i ^ bit) for i in range(lax.axis_size(axis))]
    return value + lax.ppermute(value, axis, pairs)


def with_other_three(value, axes):
    first, second, third = (
        lax.ppermute(value, axes, [(i, i ^ k) for i in range(lax.axis_size(axes))])
        for k in (1, 2, 3)
    )
    return (value + first) + (second + third)


def summed_over_z(kept, section, loss):
    half = kept.shape[0] // 8
    one_three = along_z(kept[: 4 * half].astype(SENT), -1)
    four = along_z(kept[6 * half : 7 * half].astype(SENT), -2)
    loss = with_other_three(loss, "z")
    one_three, four, loss = tied(one_three, four, loss)
    four = four.astype(F32)
    upper = kept[4 * half : 5 * half] + jnp.where(section == 0, four, 0.0)
    lower = kept[5 * half : 6 * half] + jnp.where(section == 0, 0.0, four)
    two = jnp.concatenate([upper, lower], axis=0) + one_three[2 * half :].astype(F32)
    two = along_z(two.astype(SENT), -2)
    loss = with_partner(loss, "z", 4)
    two, loss = tied(two, loss)
    two = two.astype(F32)
    given = row_half(one_three[: 2 * half], 1 - section).astype(F32) + row_half(two, 1 - section)
    got = lax.ppermute(given, "section", SWAP)
    mine = row_half(one_three[: 2 * half], section).astype(F32) + row_half(two, section)
    return kept[7 * half :] + mine + got, loss


def tower_kernel(spot, inputs, up, down, sent, own, ordered, up_held, down_held, sems):
    quarter = inputs.shape[0] // 4
    tensor = spot[0]
    step = STEP
    count = up.shape[1] // step
    loads = []
    for k, which in enumerate((1 - tensor, 3 - tensor, tensor, 2 + tensor)):
        start = pl.multiple_of(which * quarter, 16)
        rows = pl.ds(k * quarter, quarter)
        loads.append(
            pltpu.make_async_copy(
                inputs.at[pl.ds(start, quarter), :], ordered.at[rows, :], sems.at[k]
            )
        )
    for k in range(count):
        part = pl.ds(k * step, step)
        loads.append(
            pltpu.make_async_copy(up.at[:, part], up_held.at[:, part], sems.at[4 + 2 * k])
        )
        loads.append(
            pltpu.make_async_copy(down.at[part, :], down_held.at[part, :], sems.at[5 + 2 * k])
        )
    for load in loads:
        load.start()
    for load in loads[:4]:
        load.wait()
    total = jnp.zeros((4 * quarter, inputs.shape[1]), F32)
    hidden = None
    for k in range(count + 1):
        if k < count:
            loads[4 + 2 * k].wait()
        if k > 0:
            loads[3 + 2 * k].wait()
        if k < count:
            part = up_held[:, k * step : (k + 1) * step]
            coming = jnp.dot(ordered[...], part, preferred_element_type=F32)
        if k > 0:
            part = down_held[(k - 1) * step : k * step, :]
            total = total + jnp.dot(hidden, part, preferred_element_type=F32)
        if k < count:
            hidden = jax.nn.gelu(coming).astype(jnp.bfloat16)
    sent[...] = total[: 2 * quarter]
    own[...] = total[2 * quarter :] + ordered[2 * quarter :, :].astype(F32)


def tower(inputs, up, down, tensor):
    rows, width = inputs.shape
    units = up.shape[1]
    out = jax.ShapeDtypeStruct((rows // 2, width), F32)
    stays = pl.BlockSpec(memory_space=pltpu.HBM)
    sent, own = pl.pallas_call(
        tower_kernel,
        in_specs=[pl.BlockSpec(memory_space=pltpu.SMEM), stays, stays, stays],
        out_specs=[pl.BlockSpec(memory_space=pltpu.VMEM)] * 2,
        out_shape=[out, out],
        scratch_shapes=[
            pltpu.VMEM((rows, width), jnp.bfloat16),
            pltpu.VMEM((width, units), jnp.bfloat16),
            pltpu.VMEM((units, width), jnp.bfloat16),
            pltpu.SemaphoreType.DMA((4 + 2 * (units // STEP),)),
        ],
        compiler_params=pltpu.CompilerParams(vmem_limit_bytes=20 * 1024 * 1024),
        name="tower",
    )(
        jnp.reshape(tensor, (1,)).astype(jnp.int32),
        *(pltpu.with_memory_space_constraint(x, pltpu.HBM) for x in (inputs, up, down)),
    )
    raw = own + lax.ppermute(sent, "tensor", SWAP)
    norms = lax.rsqrt(jnp.sum(raw * raw, axis=-1, keepdims=True) + 1e-06)
    return (raw * norms).astype(jnp.bfloat16)


def pair_lanes(pair, tensor, quarter):
    rows = lax.dynamic_slice_in_dim(pair.reshape(2, 2, quarter), tensor, 1, 1)
    rows = rows.reshape(2 * quarter, 1)
    lane = lax.broadcasted_iota(jnp.int32, (2 * quarter, LANES), 1)
    digits = jnp.where(lane == 0, rows // LANES, jnp.where(lane == 1, rows % LANES, 0))
    return digits.astype(jnp.bfloat16)


def score_kernel(
    spot, scale, bias, own, one, three, two, four, one_other, three_other, two_other,
    four_other, reports, columns, kept, sent, report_part, loss, rows, weight, sems,
):
    count, width = reports.shape
    scale_value, bias_value = scale[0], bias[0]
    section = spot[0]
    quarter = own.shape[0] // 2
    place = 0
    groups = (
        (one, three, two, four, section),
        (one_other, three_other, two_other, four_other, 1 - section),
    )
    loads = []
    for group in groups:
        start = pl.multiple_of(group[4] * quarter, 16)
        for part in (*group[:4], own.at[pl.ds(start, quarter), :]):
            size = part.shape[0]
            held = rows.at[pl.ds(place, size), :]
            loads.append(pltpu.make_async_copy(part, held, sems.at[len(loads)]))
            place += size
    for load in loads:
        load.start()
    for load in loads:
        load.wait()

    total = jnp.zeros((1, count), F32)
    step = place // 4
    for k in range(4):
        start, stop = k * step, (k + 1) * step
        marks = rows[start:stop, width : width + 2].astype(F32)
        wanted = marks[:, 0:1] * LANES + marks[:, 1:2]
        dots = lax.dot_general(
            rows[start:stop, :width],
            reports[...],
            (((1,), (1,)), ((), ())),
            preferred_element_type=F32,
        )
        logits = scale_value * dots + bias_value
        match = wanted == columns[...]
        turned = jnp.where(match, -logits, logits)
        small = jnp.exp(-jnp.abs(turned))
        losses = jnp.maximum(turned, 0.0) + jnp.log1p(small)
        total = total + jnp.sum(losses, axis=0, keepdims=True)
        sigmoid = jnp.where(turned >= 0, 1.0, small) / (1.0 + small)
        signed = jnp.where(match, -scale_value, scale_value) * sigmoid
        weight[start:stop, :] = signed.astype(jnp.bfloat16)
    half = 2 * step
    loss[...] = jnp.broadcast_to(jnp.sum(total, axis=1, keepdims=True), loss.shape)
    kept[...] = weight[:half, :]
    sent[...] = jnp.dot(weight[half:, :], reports[...], preferred_element_type=F32)
    report_part[...] = transposed_dot(weight[...], rows[:, :width])


def scored(scale, bias, own, pieces, reports, columns):
    count, width = reports.shape
    rows = own.shape[0] + sum(piece.shape[0] for piece in pieces)
    spot = jnp.reshape(lax.axis_index("section"), (1,)).astype(jnp.int32)
    scalar = pl.BlockSpec(memory_space=pltpu.SMEM)
    whole = pl.BlockSpec(memory_space=pltpu.VMEM)
    return pl.pallas_call(
        score_kernel,
        in_specs=[scalar] * 3 + [pl.BlockSpec(memory_space=pltpu.HBM)] * 9 + [whole] * 2,
        out_specs=[whole, whole, whole, whole],
        out_shape=[
            jax.ShapeDtypeStruct((rows // 2, count), jnp.bfloat16),
            jax.ShapeDtypeStruct((rows // 2, width), F32),
            jax.ShapeDtypeStruct((count, width), F32),
            jax.ShapeDtypeStruct((1, LANES), F32),
        ],
        scratch_shapes=[
            pltpu.VMEM((rows, own.shape[1]), jnp.bfloat16),
            pltpu.VMEM((rows, count), jnp.bfloat16),
            pltpu.SemaphoreType.DMA((10,)),
        ],
        compiler_params=pltpu.CompilerParams(vmem_limit_bytes=12 * 1024 * 1024),
        name="scores",
    )(
        spot,
        scale,
        bias,
        *(pltpu.with_memory_space_constraint(x, pltpu.HBM) for x in (own, *pieces)),
        reports,
        columns,
    )


def transposed_dot(weight, slides):
    return lax.dot_general(weight, slides, (((0,), (0,)), ((), ())), preferred_element_type=F32)


def local(tower_input, up_weight, down_weight, pair, scale, bias):
    section = lax.axis_index("section")
    tensor = lax.axis_index("tensor")
    n_z = lax.axis_size("z")
    n_plane = lax.axis_size(PLANE)
    quarter, width = tower_input.shape[1] // 4, tower_input.shape[2]
    total = lax.axis_size(ALL) * quarter

    lanes = pair_lanes(pair, tensor, quarter)
    embedded = tower(tower_input[0], up_weight[0], down_weight[0], tensor)
    swapped = lax.ppermute(embedded, "section", SWAP)
    slides = jnp.concatenate([jnp.where(section == 0, embedded, swapped), lanes], axis=1)
    reports = row_half(jnp.where(section == 0, swapped, embedded), section)

    repeated = jnp.broadcast_to(reports, (n_plane, *reports.shape))
    repeated, slides = tied(repeated, slides)
    reports_all = exchanged(repeated, PLANE).reshape(n_plane * quarter, -1)
    pieces = gathered_over_z(slides, section)

    place = jnp.arange(n_plane * quarter, dtype=jnp.int32)
    member, row = place // quarter, place % quarter
    owner = ((member // 2 * n_z + lax.axis_index("z")) * 2 + section) * 2 + member % 2
    columns = (owner * quarter + row).astype(F32)

    weight, sent, report_part, loss = scored(
        scale, bias, slides, pieces, reports_all, columns[None, :]
    )
    back = lax.ppermute(sent, "section", SWAP)
    loss = with_other_three(loss, ("xl", "tensor"))
    report_part = report_part.astype(SENT).reshape(n_plane, quarter, width)
    report_part, loss, weight = tied(report_part, loss, weight)
    report_terms = exchanged(report_part, PLANE)
    loss = with_partner(loss, "section", 1)
    back, loss = tied(back, loss)
    kept = jnp.dot(weight, reports_all, preferred_element_type=F32) + back
    slide_grad, loss = summed_over_z(kept, section, loss)
    report_terms, loss = tied(report_terms, loss)
    report_grad = report_terms.astype(F32).sum(axis=0)
    loss, report_grad = tied(with_other_three(loss, "y"), report_grad)
    return (loss[0, :1] / total, slide_grad, report_grad)


def solution(mesh):
    finer = Mesh(
        mesh.devices.reshape(2, 4, 8, mesh.shape["section"], mesh.shape["tensor"]),
        ALL,
    )
    return jax.shard_map(
        local,
        mesh=finer,
        in_specs=(
            P("section", DP, None),
            P("section", None, "tensor"),
            P("section", "tensor", None),
            P(DP),
            P(),
            P(),
        ),
        out_specs=(P(), P(ALL, None), P(ALL, None)),
        check_vma=False,
    )
```
